1024 devices in a mesh: sec: 2 (over core), grp: 16 (over x, y), blk: 32 (over z).
Axes of the slice: x: 4, y: 4, z: 32, core: 2. Of those that a mesh axis runs over, the one named last changes fastest.
Arguments:
- atm_flux: bfloat16 [2, 60, 2097152], P(None, None, ('sec', 'grp', 'blk')), may hold values from -25 to 25
- tile_bank: bfloat16 [128, 128, 128], replicated, may hold values from -1 to 1
- pair_count: int32 [1024], P(('sec', 'grp', 'blk')), may hold values from 32 to 128, as said below
- pair_source: int32 [131072], P(('sec', 'grp', 'blk')), may hold values from 0 to 15
- pair_tile: int32 [131072], P(('sec', 'grp', 'blk')), may hold values from 0 to 127
- pair_target: int32 [131072], P(('sec', 'grp', 'blk')), may hold values from 0 to 63
- tracers: bfloat16 [32, 60, 262144], P(None, None, ('sec', 'grp', 'blk')), may hold values from -6 to 6
- diffusivity: float32 [31, 262144], P(None, ('sec', 'grp', 'blk')), may hold values from 0.2 to 5
- column_depth: int32 [262144], P(('sec', 'grp', 'blk')), may hold values from 0 to 32
Outputs:
- mixed_tracers: float32 [32, 60, 262144], P(None, None, ('sec', 'grp', 'blk'))
The draws below stay inside these ranges and needn't reach their ends.
Inputs may be any that keep to these rules, and one draw needn't show every extreme that they name: `pair_count`: pairs at positions 127 and below that are at or past a device's count are unused; some device has exactly 128 live pairs. `pair_target`: a target t names ocean block t % 2 of the device at blk index t // 2 with the same sec and grp. Levels at index column_depth and below are dry; 0 marks a land column.
All inputs are finite; a program needn't handle non-finite values.
Results may differ from the reference program's by a relative error of at most 0.013.
Values may be sent and summed in bfloat16 or wider, within the bound.
No kernel may reach another device: no remote copies, remote signals or barrier semaphores. Data moves between devices by JAX's collectives and lax.ppermute only.
A program may use at most 64 MiB of HBM per device.

```python
import math
import jax
import jax.numpy as jnp
from jax import lax

FIELDS = 60
TILE = 128
SUB = 2
SRC_BLOCKS = 16
PAIRS = 128
OCN_BLOCKS = 2
LEVELS = 32
BANK = 128
DEVICE_COUNT = 1024
ATM_ROWS = 2097152
NCOL = 262144
TARGETS = 64
N_BLK = 32


def draw_atm_flux(key, part):
    rough_key, mean_key = jax.random.split(jax.random.fold_in(key, 11))
    position = jnp.arange(ATM_ROWS, dtype=jnp.float32) / ATM_ROWS
    rising = 1.0 + 2.0 * position
    rough_part = jnp.clip(jax.random.normal(rough_key, (SUB, FIELDS, ATM_ROWS), jnp.float32), -4.0, 4.0)
    field_mean = jax.random.uniform(mean_key, (SUB, FIELDS, 1), jnp.float32, 0.2, 0.6)
    return (rising[None, None, :] * (field_mean + rough_part)).astype(jnp.bfloat16)


def draw_tile_bank(key, part):
    spread = (PAIRS * TILE / 8.0) ** (-0.5)
    offset_mean = 4.0 / (PAIRS * TILE)
    tile_key = jax.random.fold_in(key, 23)
    rough_part = jnp.clip(jax.random.normal(tile_key, (BANK, TILE, TILE), jnp.float32), -4.0, 4.0)
    return (rough_part * spread + offset_mean).astype(jnp.bfloat16)


def draw_pair_count(key, part):
    first_key, second_key, full_key = jax.random.split(jax.random.fold_in(key, 37), 3)
    first_draw = jax.random.randint(first_key, (DEVICE_COUNT,), 0, PAIRS)
    second_draw = jax.random.randint(second_key, (DEVICE_COUNT,), 0, PAIRS)
    counts = PAIRS // 4 + 3 * first_draw * second_draw // (4 * PAIRS)
    full_device = jax.random.randint(full_key, (), 0, DEVICE_COUNT)
    light_device = (full_device + 1) % DEVICE_COUNT
    device_ids = jnp.arange(DEVICE_COUNT, dtype=jnp.int32)
    counts = jnp.where(device_ids == light_device, PAIRS // 4, counts)
    return jnp.where(device_ids == full_device, PAIRS, counts).astype(jnp.int32)


def place_ends(values, key, low, largest):
    dims = values.shape
    index_at = [jax.random.randint(jax.random.fold_in(key, axis), (), 0, dims[axis]) for axis in range(len(dims))]
    values = values.at[tuple(index_at)].set(low)
    longest = dims.index(max(dims))
    index_at[longest] = (index_at[longest] + 1) % dims[longest]
    return values.at[tuple(index_at)].set(largest)


def levels(rng, extent, shards, least, largest):
    level = 1.0
    for axis_at, blocks in shards:
        draws = jax.random.uniform(jax.random.fold_in(jax.random.fold_in(rng, 6), axis_at), (blocks,), jnp.float32, least / len(shards), largest / len(shards))
        level = level * jnp.repeat(jnp.exp(draws), extent[axis_at] // blocks).reshape((-1,) + (1,) * (len(extent) - 1 - axis_at))
    return level


def normal_values(stream_key, dims, scale, most, shards=(), held_as=jnp.bfloat16):
    values = jax.random.normal(stream_key, dims, jnp.float32) * scale
    if len(shards) > 0:
        values = levels(stream_key, dims, shards, -0.22, 0.18) * values
    return jnp.clip(values, min=-most, max=most).astype(held_as)


def setup_inputs(seed: int = 0) -> dict:
    streams_of = jax.random.split(jax.random.key(seed), 10)
    atm_flux = draw_atm_flux(jax.random.fold_in(streams_of[9], 71), 0)
    tile_bank = draw_tile_bank(jax.random.fold_in(streams_of[9], 71), 0)
    pair_count = draw_pair_count(jax.random.fold_in(streams_of[9], 71), 0)
    pair_source = place_ends(jax.random.randint(streams_of[3], (DEVICE_COUNT * PAIRS,), 0, SRC_BLOCKS), jax.random.fold_in(streams_of[3], 1), 0, SRC_BLOCKS - 1).astype(jnp.int32)
    pair_tile = place_ends(jax.random.randint(streams_of[4], (DEVICE_COUNT * PAIRS,), 0, BANK), jax.random.fold_in(streams_of[4], 1), 0, BANK - 1).astype(jnp.int32)
    pair_target = place_ends(jax.random.randint(streams_of[5], (DEVICE_COUNT * PAIRS,), 0, TARGETS), jax.random.fold_in(streams_of[5], 1), 0, TARGETS - 1).astype(jnp.int32)
    tracers = normal_values(streams_of[6], (LEVELS, FIELDS, NCOL), 1.0, 6.0, ((2, 1024),))
    diffusivity = jnp.clip(jnp.exp(math.log(5.0) - 3.218876 * jax.random.uniform(streams_of[7], (LEVELS - 1, NCOL), jnp.float32) ** levels(streams_of[7], (LEVELS - 1, NCOL), ((1, 1024),), -0.2, 0.2)), 0.2, 5.0)
    column_depth = place_ends(jax.random.randint(streams_of[8], (NCOL,), 0, LEVELS + 1), jax.random.fold_in(streams_of[8], 1), 0, LEVELS).astype(jnp.int32)
    return dict(atm_flux=atm_flux, tile_bank=tile_bank, pair_count=pair_count, pair_source=pair_source, pair_tile=pair_tile, pair_target=pair_target, tracers=tracers, diffusivity=diffusivity, column_depth=column_depth)


def column_factors(diffusivity, column_depth):
    layer_count = diffusivity.shape[0] + 1
    layer_ids = jnp.arange(layer_count, dtype=jnp.int32)
    active = layer_ids[:, None] < column_depth[None, :]
    interior = diffusivity * active[1:].astype(diffusivity.dtype)
    boundary = jnp.zeros_like(diffusivity[:1])
    coupling = jnp.concatenate([boundary, interior, boundary], axis=0)
    diagonal = 1.0 + coupling[:-1] + coupling[1:]
    inverse_pivot = []
    upper_ratio = []
    for k in range(layer_count):
        if k == 0:
            pivot_entry = diagonal[0]
        else:
            pivot_entry = diagonal[k] + coupling[k] * upper_ratio[k - 1]
        inverse = 1.0 / pivot_entry
        inverse_pivot.append(inverse)
        upper_ratio.append(-coupling[k + 1] * inverse)
    live_mask = active.astype(diffusivity.dtype)[:, None, :]
    surface = (column_depth > 0).astype(diffusivity.dtype)
    return coupling, inverse_pivot, upper_ratio, live_mask, surface


def mix_once(column_state, surface_term, factors):
    coupling, inverse_pivot, upper_ratio, live_mask, surface = factors
    right_side = column_state.at[0].add(surface_term * surface[None, :]) * live_mask
    forward = []
    for k in range(right_side.shape[0]):
        if k == 0:
            carried = right_side[0]
        else:
            carried = right_side[k] + coupling[k][None, :] * forward[k - 1]
        forward.append(carried * inverse_pivot[k][None, :])
    solved = [forward[-1]]
    for k in range(right_side.shape[0] - 2, -1, -1):
        solved.append(forward[k] - upper_ratio[k][None, :] * solved[-1])
    return jnp.stack(solved[::-1])


def remap_device(flux_blocks, live_count, sources, tile_ids, targets, tile_bank):
    picked = jnp.take(flux_blocks, sources, axis=1).astype(jnp.float32)
    chosen = jnp.take(tile_bank, tile_ids, axis=0).astype(jnp.float32)
    products = jnp.einsum("spr,prc->psc", picked, chosen)
    live_pairs = (jnp.arange(PAIRS, dtype=jnp.int32) < live_count).astype(jnp.float32)
    products = products * live_pairs[:, None, None]
    zero_sums = jnp.zeros((N_BLK, SUB * FIELDS, OCN_BLOCKS, TILE), jnp.float32)
    summed = zero_sums.at[targets // OCN_BLOCKS, :, targets % OCN_BLOCKS].add(products)
    return summed.astype(jnp.bfloat16)


def reference(atm_flux, tile_bank, pair_count, pair_source, pair_tile, pair_target, tracers, diffusivity, column_depth):
    stacked = SUB * FIELDS
    group_count = DEVICE_COUNT // N_BLK
    blocks = atm_flux.reshape(stacked, DEVICE_COUNT, SRC_BLOCKS, TILE).transpose(1, 0, 2, 3)
    blocks = blocks.reshape(group_count, N_BLK, stacked, SRC_BLOCKS, TILE)

    def shaped(a):
        return a.reshape(group_count, N_BLK, PAIRS)

    def one_group(group_args):
        flux_group, counts, sources, tile_ids, targets = group_args

        def one_device(device_args):
            return remap_device(*device_args, tile_bank)

        outgoing = lax.map(one_device, (flux_group, counts, sources, tile_ids, targets))
        received = jnp.sum(outgoing.astype(jnp.float32), axis=0)
        ocean_part = jnp.sum(received, axis=(0, 2, 3))
        atm_part = jnp.sum(flux_group.astype(jnp.float32), axis=(0, 2, 3))
        return received, atm_part, ocean_part

    received, atm_parts, ocean_parts = lax.map(
        one_group,
        (blocks, pair_count.reshape(group_count, N_BLK), shaped(pair_source), shaped(pair_tile), shaped(pair_target)))
    device_width = OCN_BLOCKS * TILE
    forcing_all = received.reshape(DEVICE_COUNT, SUB, FIELDS, device_width)
    atm_total = jnp.sum(atm_parts, axis=0).reshape(SUB, FIELDS)
    ocean_total = jnp.sum(ocean_parts, axis=0).reshape(SUB, FIELDS)
    correction = (atm_total * (OCN_BLOCKS / SRC_BLOCKS) - ocean_total) / NCOL

    def mix_device(device_index, result):
        first_column = jnp.asarray(device_index * device_width).astype(jnp.int32)
        column_state = lax.dynamic_slice_in_dim(tracers, first_column, device_width, 2).astype(jnp.float32)
        factors = column_factors(
            lax.dynamic_slice_in_dim(diffusivity, first_column, device_width, 1),
            lax.dynamic_slice_in_dim(column_depth, first_column, device_width, 0))
        for substep in range(SUB):
            column_state = mix_once(column_state, forcing_all[device_index, substep] + correction[substep][:, None], factors)
        return lax.dynamic_update_slice_in_dim(result, column_state, first_column, 2)

    return lax.fori_loop(0, DEVICE_COUNT, mix_device, jnp.zeros((LEVELS, FIELDS, NCOL), jnp.float32))
```

```python
import jax
import jax.numpy as jnp
from jax import lax
from jax.experimental import pallas as pl
from jax.experimental.pallas import tpu as pltpu
from jax.sharding import PartitionSpec as P

F32 = jnp.float32
BF16 = jnp.bfloat16
HALF = 64
ROWS = 128
TILE = 128
UNROLL = 4


def remap_kernel(count_ref, me_ref, source_ref, tile_ref, target_ref, flux_ref, bank_ref,
                 out_ref, part_ref, blocks, acc):
    subs, fields, atm_rows = flux_ref.shape
    source_blocks = atm_rows // TILE
    slots = out_ref.shape[1]
    blocks[...] = jnp.zeros(blocks.shape, BF16)
    atm = jnp.zeros((ROWS, TILE), F32)
    for s in range(source_blocks):
        for sub in range(subs):
            blocks[s, pl.ds(sub * HALF, fields)] = flux_ref[sub, :, pl.ds(s * TILE, TILE)]
        atm = atm + blocks[s].astype(F32)
    acc[...] = jnp.zeros(acc.shape, F32)
    count = count_ref[0]
    me = me_ref[0]

    def slot_of(p):
        target = target_ref[p]
        half = target & 1
        owner = target >> 1
        r = jnp.where(half == 0, owner - me, me - owner) & (slots - 1)
        r1 = r & 1
        r2 = (r >> 1) & 3
        r3 = ((r >> 3) + jnp.where(r2 == 3, 1, 0)) & 3
        place = half * slots + r1 * 16 + r2 * 4 + r3
        return jnp.where(p < count, place, 2 * slots)

    def group(g, carry):
        terms = []
        for j in range(UNROLL):
            p = g * UNROLL + j
            terms.append(jnp.dot(blocks[source_ref[p]], bank_ref[tile_ref[p]],
                                 preferred_element_type=F32))
        for j in range(UNROLL):
            place = slot_of(g * UNROLL + j)
            acc[place] = acc[place] + terms[j]
        return carry

    lax.fori_loop(0, (count + UNROLL - 1) // UNROLL, group, 0)

    def flush(i, ocean):
        for half in range(2):
            sent = acc[half * slots + i].astype(BF16)
            out_ref[half, i] = sent
            ocean = ocean + sent.astype(F32)
        return ocean

    ocean = lax.fori_loop(0, slots, flush, jnp.zeros((ROWS, TILE), F32), unroll=4)
    share = 2.0 * TILE / atm_rows
    part = atm * share - ocean
    part_ref[...] = lax.dot_general(jnp.ones((8, TILE), F32), part, (((1,), (1,)), ((), ())),
                                    precision=lax.Precision.HIGHEST, preferred_element_type=F32)


def remap(pair_count, me, pair_source, pair_tile, pair_target, flux, bank, slots):
    smem = pl.BlockSpec(memory_space=pltpu.SMEM)
    vmem = pl.BlockSpec(memory_space=pltpu.VMEM)
    source_blocks = flux.shape[2] // TILE
    return pl.pallas_call(
        remap_kernel,
        out_shape=(jax.ShapeDtypeStruct((2, slots, ROWS, TILE), BF16),
                   jax.ShapeDtypeStruct((8, ROWS), F32)),
        in_specs=[smem] * 5 + [vmem, vmem],
        out_specs=(vmem, vmem),
        scratch_shapes=[pltpu.VMEM((source_blocks, ROWS, TILE), BF16),
                        pltpu.VMEM((2 * slots + 1, ROWS, TILE), F32)],
        compiler_params=pltpu.CompilerParams(vmem_limit_bytes=40 << 20),
        cost_estimate=pl.CostEstimate(flops=2 * 128 * 128 ** 3, transcendentals=0,
                                      bytes_accessed=8 << 20),
        name="remap",
    )(pair_count, me, pair_source, pair_tile, pair_target, flux, bank)


def mix_kernel(tracer_ref, diff_ref, depth_ref, state_ref, unit_ref, ahead, lower, upper):
    levels, fields, columns = tracer_ref.shape
    depth = depth_ref[...]
    zero = jnp.zeros((1, columns), F32)
    one = jnp.ones((1, columns), F32)

    def coupling(k):
        if k == 0 or k == levels:
            return zero
        return jnp.where(depth > k, diff_ref[pl.ds(k - 1, 1), :], zero)

    ratio = None
    for k in range(levels):
        a, b = coupling(k), coupling(k + 1)
        pivot = 1.0 + a + b
        if k > 0:
            pivot = pivot - a * ratio
        inverse = 1.0 / pivot
        ratio = b * inverse
        wet = jnp.where(depth > k, one, zero)
        ahead[pl.ds(k, 1), :] = wet * inverse
        lower[pl.ds(k, 1), :] = a * inverse
        upper[pl.ds(k, 1), :] = ratio
    unit = [jnp.where(depth > 0, one, zero)] + [zero] * (levels - 1)
    for sweep in range(2):
        carried = None
        unit_carried = None
        for k in range(levels):
            if sweep == 0:
                x = tracer_ref[k].astype(F32)
            else:
                x = state_ref[k]
            scale = ahead[pl.ds(k, 1), :]
            below = lower[pl.ds(k, 1), :]
            if k == 0:
                carried = x * scale
                unit_carried = unit[k] * scale
            else:
                carried = x * scale + carried * below
                unit_carried = unit[k] * scale + unit_carried * below
            state_ref[k] = carried
            unit[k] = unit_carried
        for k in range(levels - 2, -1, -1):
            above = upper[pl.ds(k, 1), :]
            carried = state_ref[k] + carried * above
            state_ref[k] = carried
            unit[k] = unit[k] + unit[k + 1] * above
        for k in range(levels):
            unit_ref[sweep, pl.ds(k, 1), :] = unit[k]


def mix(tracers, diffusivity, column_depth):
    levels, fields, columns = tracers.shape
    vmem = pl.BlockSpec(memory_space=pltpu.VMEM)
    return pl.pallas_call(
        mix_kernel,
        out_shape=(jax.ShapeDtypeStruct((levels, fields, columns), F32),
                   jax.ShapeDtypeStruct((2, levels, columns), F32)),
        in_specs=[vmem] * 3,
        out_specs=(vmem, vmem),
        scratch_shapes=[pltpu.VMEM((levels, columns), F32)] * 3,
        compiler_params=pltpu.CompilerParams(vmem_limit_bytes=24 << 20),
        cost_estimate=pl.CostEstimate(flops=12 * levels * fields * columns, transcendentals=0,
                                      bytes_accessed=6 * levels * fields * columns),
        name="mix",
    )(tracers, diffusivity, column_depth.reshape(1, columns))


def finish_kernel(state_ref, unit_ref, own_ref, near_ref, back_ref, far_ref, total_ref, out_ref):
    levels, fields, columns = state_ref.shape
    eye = (lax.broadcasted_iota(jnp.int32, (ROWS, ROWS), 0)
           == lax.broadcasted_iota(jnp.int32, (ROWS, ROWS), 1))
    spread = jnp.where(eye, jnp.broadcast_to(total_ref[...], (ROWS, ROWS)), 0.0)
    fix = jnp.sum(spread, axis=1, keepdims=True)
    for o in range(2):
        lanes = pl.ds(o * TILE, TILE)
        surface = (own_ref[o] + near_ref[o].astype(F32) + back_ref[o].astype(F32)
                   + far_ref[o].astype(F32)) + fix
        first = surface[0:fields]
        second = surface[HALF:HALF + fields]
        for k in range(levels):
            out_ref[k, :, lanes] = (state_ref[k, :, lanes]
                                    + first * unit_ref[1, pl.ds(k, 1), lanes]
                                    + second * unit_ref[0, pl.ds(k, 1), lanes])


def finish(state, unit, own, near, back, far, total):
    vmem = pl.BlockSpec(memory_space=pltpu.VMEM)
    return pl.pallas_call(
        finish_kernel,
        out_shape=jax.ShapeDtypeStruct(state.shape, F32),
        in_specs=[vmem] * 7,
        out_specs=vmem,
        input_output_aliases={0: 0},
        compiler_params=pltpu.CompilerParams(vmem_limit_bytes=24 << 20),
        name="finish",
    )(state, unit, own, near, back, far, total)


def shift(x, by, ring):
    return lax.ppermute(x, "blk", [(i, (i + by) % ring) for i in range(ring)])


def pieces(total):
    high = lax.reduce_precision(total, 8, 7)
    middle = lax.reduce_precision(total - high, 8, 7)
    low = total - high - middle
    return jnp.stack([high, middle, low])


def with_total(chunks, total):
    row = lax.broadcasted_iota(jnp.int32, chunks.shape, chunks.ndim - 2)
    parts = pieces(total)
    for i in range(3):
        chunks = jnp.where(row == HALF - 4 + i, parts[i], chunks)
    return chunks


def total_in(chunk):
    rows = chunk[HALF - 4:HALF - 1].astype(F32)
    return rows[0] + rows[1] + rows[2]


def exchange(sums, total, step, ring):
    sent = [with_total(sums[0], total).astype(BF16), sums[1].astype(BF16)]
    near = shift(jnp.stack([sent[0][1], sent[1][3]]), step, ring)
    back = shift(jnp.stack([sent[0][3], sent[1][1]]), -step, ring)
    if 4 * step == ring:
        far = shift(jnp.stack([sent[0][2], sent[1][2]]), 2 * step, ring)
    else:
        far = jnp.stack([shift(sent[0][2], 2 * step, ring), shift(sent[1][2], -2 * step, ring)])
    return near, back, far


def body(
    atm_flux,
    tile_bank,
    pair_count,
    pair_source,
    pair_tile,
    pair_target,
    tracers,
    diffusivity,
    column_depth,
):
    ring = lax.axis_size("blk")
    plane = lax.axis_size("sec") * lax.axis_size("grp")
    columns = tracers.shape[2]
    me = lax.axis_index("blk").astype(jnp.int32).reshape(1)
    chunks, part = remap(pair_count, me, pair_source, pair_tile, pair_target, atm_flux, tile_bank,
                         ring)
    gathered = lax.all_to_all(jnp.broadcast_to(part[:1], (plane, ROWS)), ("sec", "grp"), 0, 0,
                              tiled=True)
    total = jnp.sum(gathered, axis=0)
    total = total + shift(total, 1, ring)
    chunks = chunks.reshape(2, 2, 4, 4, ROWS, TILE)
    arrived = [shift(chunks[0, 1], 1, ring), shift(chunks[1, 1], -1, ring)]
    state, unit = mix(tracers, diffusivity, column_depth)
    sums = [chunks[o, 0].astype(F32) + arrived[o].astype(F32) for o in range(2)]
    near, back, far = exchange(sums, total, 2, ring)
    total = total + total_in(near[0, 0]) + total_in(back[0, 0]) + total_in(far[0, 0])
    sums = [sums[o][0] + near[o].astype(F32) + back[o].astype(F32) + far[o].astype(F32)
            for o in range(2)]
    near, back, far = exchange(sums, total, 8, ring)
    total = total + total_in(near[0]) + total_in(back[0]) + total_in(far[0])
    own = jnp.stack([sums[0][0], sums[1][0]])
    fix = total / (columns * ring * plane)
    return finish(state, unit, own, near, back, far, fix.reshape(1, ROWS))


def solution(mesh):
    placed = (
        P(None, None, ("sec", "grp", "blk")),
        P(),
        P(("sec", "grp", "blk")),
        P(("sec", "grp", "blk")),
        P(("sec", "grp", "blk")),
        P(("sec", "grp", "blk")),
        P(None, None, ("sec", "grp", "blk")),
        P(None, ("sec", "grp", "blk")),
        P(("sec", "grp", "blk")),
    )
    return jax.shard_map(
        body,
        mesh=mesh,
        in_specs=placed,
        out_specs=P(None, None, ("sec", "grp", "blk")),
        check_vma=False,
    )
```

```python
import functools

import jax
import jax.numpy as jnp
from jax import lax
from jax.experimental import pallas as pl
from jax.experimental.pallas import tpu as pltpu
from jax.sharding import PartitionSpec as P

F32 = jnp.float32
BF16 = jnp.bfloat16
HALF = 64
ROWS = 128
TILE = 128
UNROLL = 4
BANK_COPIES = 8
FIELD_CHUNK = 15


def remap_kernel(count_ref, me_ref, source_hbm, tile_hbm, target_hbm, flux_ref, bank_hbm,
                 right_ref, left_ref, keep_ref, part_ref,
                 source_ref, tile_ref, target_ref, bank_ref, blocks, acc, list_sem, bank_sem):
    subs, fields, atm_rows = flux_ref.shape
    source_blocks = atm_rows // TILE
    sent_slots = right_ref.shape[0]
    slots = 2 * sent_slots
    lists = [pltpu.make_async_copy(src, dst, list_sem.at[i]) for i, (src, dst) in enumerate(
        ((source_hbm, source_ref), (tile_hbm, tile_ref), (target_hbm, target_ref)))]
    span = bank_ref.shape[0] // BANK_COPIES
    loads = [pltpu.make_async_copy(bank_hbm.at[pl.ds(i * span, span)],
                                   bank_ref.at[pl.ds(i * span, span)], bank_sem.at[i])
             for i in range(BANK_COPIES)]
    for copy in lists + loads:
        copy.start()
    blocks[...] = jnp.zeros(blocks.shape, BF16)
    atm = jnp.zeros((ROWS, TILE), F32)
    for s in range(source_blocks):
        for sub in range(subs):
            blocks[s, pl.ds(sub * HALF, fields)] = flux_ref[sub, :, pl.ds(s * TILE, TILE)]
        atm = atm + blocks[s].astype(F32)
    acc[...] = jnp.zeros(acc.shape, F32)
    count = count_ref[0]
    me = me_ref[0]
    for copy in lists + loads:
        copy.wait()

    def slot_of(p):
        target = target_ref[p]
        half = target & 1
        owner = target >> 1
        r = jnp.where(half == 0, owner - me, me - owner) & (slots - 1)
        r1 = r & 1
        r2 = (r >> 1) & 3
        r3 = ((r >> 3) + jnp.where(r2 == 3, 1, 0)) & 3
        place = half * slots + r1 * sent_slots + r2 * 4 + r3
        return jnp.where(p < count, place, 2 * slots)

    def group(g, carry):
        terms = []
        for j in range(UNROLL):
            p = g * UNROLL + j
            terms.append(jnp.dot(blocks[source_ref[p]], bank_ref[tile_ref[p]],
                                 preferred_element_type=F32))
        for j in range(UNROLL):
            place = slot_of(g * UNROLL + j)
            acc[place] = acc[place] + terms[j]
        return carry

    lax.fori_loop(0, (count + UNROLL - 1) // UNROLL, group, 0)

    def flush(i, ocean):
        for half in range(2):
            kept = acc[half * slots + i].astype(BF16)
            sent = acc[half * slots + sent_slots + i].astype(BF16)
            keep_ref[half, i] = kept
            if half == 0:
                right_ref[i] = sent
            else:
                left_ref[i] = sent
            ocean = ocean + kept.astype(F32) + sent.astype(F32)
        return ocean

    ocean = lax.fori_loop(0, sent_slots, flush, jnp.zeros((ROWS, TILE), F32), unroll=4)
    share = 2.0 * TILE / atm_rows
    part = atm * share - ocean
    part_ref[...] = lax.dot_general(jnp.ones((8, TILE), F32), part, (((1,), (1,)), ((), ())),
                                    precision=lax.Precision.HIGHEST, preferred_element_type=F32)


def remap(pair_count, me, pair_source, pair_tile, pair_target, flux, bank, slots):
    smem = pl.BlockSpec(memory_space=pltpu.SMEM)
    vmem = pl.BlockSpec(memory_space=pltpu.VMEM)
    hbm = pl.BlockSpec(memory_space=pltpu.HBM)
    source_blocks = flux.shape[2] // TILE
    half = slots // 2
    return pl.pallas_call(
        remap_kernel,
        out_shape=(jax.ShapeDtypeStruct((half, ROWS, TILE), BF16),
                   jax.ShapeDtypeStruct((half, ROWS, TILE), BF16),
                   jax.ShapeDtypeStruct((2, half, ROWS, TILE), BF16),
                   jax.ShapeDtypeStruct((8, ROWS), F32)),
        in_specs=[smem] * 2 + [hbm] * 3 + [vmem, hbm],
        out_specs=(vmem,) * 4,
        scratch_shapes=[pltpu.SMEM(pair_source.shape, jnp.int32)] * 3
        + [pltpu.VMEM(bank.shape, BF16),
           pltpu.VMEM((source_blocks, ROWS, TILE), BF16),
           pltpu.VMEM((2 * slots + 1, ROWS, TILE), F32),
           pltpu.SemaphoreType.DMA((3,)),
           pltpu.SemaphoreType.DMA((BANK_COPIES,))],
        compiler_params=pltpu.CompilerParams(vmem_limit_bytes=40 << 20),
        cost_estimate=pl.CostEstimate(flops=2 * 128 * 128 ** 3, transcendentals=0,
                                      bytes_accessed=8 << 20),
        name="remap",
    )(pair_count, me, *(pltpu.with_memory_space_constraint(x, pltpu.HBM)
                        for x in (pair_source, pair_tile, pair_target)), flux,
      pltpu.with_memory_space_constraint(bank, pltpu.HBM))


def combine_kernel(keep_ref, right_ref, left_ref, own_ref, near_ref, back_ref, far_ref, other_ref):
    for code in range(4):
        for i in range(4):
            place = code * 4 + i
            first = keep_ref[0, place].astype(F32) + right_ref[place].astype(F32)
            second = keep_ref[1, place].astype(F32) + left_ref[place].astype(F32)
            if code == 0:
                own_ref[0, i] = first
                own_ref[1, i] = second
            elif code == 1:
                near_ref[0, i] = first.astype(BF16)
                back_ref[1, i] = second.astype(BF16)
            elif code == 3:
                back_ref[0, i] = first.astype(BF16)
                near_ref[1, i] = second.astype(BF16)
            else:
                far_ref[i] = first.astype(BF16)
                other_ref[i] = second.astype(BF16)


def combine(keep, right, left):
    vmem = pl.BlockSpec(memory_space=pltpu.VMEM)
    pair = jax.ShapeDtypeStruct((2, 4, ROWS, TILE), BF16)
    single = jax.ShapeDtypeStruct((4, ROWS, TILE), BF16)
    return pl.pallas_call(
        combine_kernel,
        out_shape=(jax.ShapeDtypeStruct((2, 4, ROWS, TILE), F32), pair, pair, single, single),
        in_specs=[vmem] * 3,
        out_specs=(vmem,) * 5,
        compiler_params=pltpu.CompilerParams(vmem_limit_bytes=16 << 20),
        name="combine",
    )(keep, right, left)


def with_total(chunk, total):
    row = lax.broadcasted_iota(jnp.int32, chunk.shape, 0)
    for i in range(3):
        piece = total.astype(BF16).astype(F32)
        chunk = jnp.where(row == HALF - 4 + i, piece, chunk)
        total = total - piece
    return chunk.astype(BF16)


def total_in(chunk):
    rows = chunk.astype(F32)
    place = HALF - 4
    return rows[place:place + 1] + rows[place + 1:place + 2] + rows[place + 2:place + 3]


def gather_kernel(own_ref, near_ref, back_ref, far_ref, other_ref, total_ref,
                  outer_ref, mirror_ref, rest_ref):
    for o in range(2):
        for at, code in enumerate((2, 0, 1, 3)):
            last = (far_ref, other_ref)[o]
            value = (own_ref[o, code] + near_ref[o, code].astype(F32)
                     + back_ref[o, code].astype(F32) + last[code].astype(F32))
            if at > 0:
                rest_ref[o, at - 1] = value
            elif o == 0:
                outer_ref[...] = with_total(value, total_ref[...])
            else:
                mirror_ref[...] = value.astype(BF16)


def gather(own, near, back, far, other, total):
    vmem = pl.BlockSpec(memory_space=pltpu.VMEM)
    chunk = jax.ShapeDtypeStruct((ROWS, TILE), BF16)
    return pl.pallas_call(
        gather_kernel,
        out_shape=(chunk, chunk, jax.ShapeDtypeStruct((2, 3, ROWS, TILE), F32)),
        in_specs=[vmem] * 6,
        out_specs=(vmem,) * 3,
        compiler_params=pltpu.CompilerParams(vmem_limit_bytes=16 << 20),
        name="gather",
    )(own, near, back, far, other, total)


def relay_kernel(rest_ref, outer_ref, mirror_ref, total_ref, near_ref, back_ref):
    total = total_ref[...]
    near_ref[0] = with_total(rest_ref[0, 1] + outer_ref[...].astype(F32),
                             total + total_in(outer_ref[...]))
    near_ref[1] = rest_ref[1, 2].astype(BF16)
    back_ref[0] = with_total(rest_ref[0, 2], total)
    back_ref[1] = (rest_ref[1, 1] + mirror_ref[...].astype(F32)).astype(BF16)


def relay(rest, outer, mirror, total):
    vmem = pl.BlockSpec(memory_space=pltpu.VMEM)
    pair = jax.ShapeDtypeStruct((2, ROWS, TILE), BF16)
    return pl.pallas_call(
        relay_kernel,
        out_shape=(pair, pair),
        in_specs=[vmem] * 4,
        out_specs=(vmem,) * 2,
        compiler_params=pltpu.CompilerParams(vmem_limit_bytes=16 << 20),
        name="relay",
    )(rest, outer, mirror, total)


def mix_kernel(tracer_ref, diff_ref, depth_ref, solved_ref, unit_ref, state_ref, ahead, lower, upper):
    levels, fields, columns = tracer_ref.shape
    depth = depth_ref[...]
    zero = jnp.zeros((1, columns), F32)
    one = jnp.ones((1, columns), F32)

    def coupling(k):
        if k == 0 or k == levels:
            return zero
        return jnp.where(depth > k, diff_ref[pl.ds(k - 1, 1), :], zero)

    ratio = None
    for k in range(levels):
        a, b = coupling(k), coupling(k + 1)
        pivot = 1.0 + a + b
        if k > 0:
            pivot = pivot - a * ratio
        inverse = 1.0 / pivot
        ratio = b * inverse
        wet = jnp.where(depth > k, one, zero)
        ahead[pl.ds(k, 1), :] = wet * inverse
        lower[pl.ds(k, 1), :] = a * inverse
        upper[pl.ds(k, 1), :] = ratio
    unit = [jnp.where(depth > 0, one, zero)] + [zero] * (levels - 1)
    for sweep in range(2):
        carried = None
        unit_carried = None
        for k in range(levels):
            if sweep == 0:
                x = tracer_ref[k].astype(F32)
            else:
                x = state_ref[k]
            scale = ahead[pl.ds(k, 1), :]
            below = lower[pl.ds(k, 1), :]
            if k == 0:
                carried = x * scale
                unit_carried = unit[k] * scale
            else:
                carried = x * scale + carried * below
                unit_carried = unit[k] * scale + unit_carried * below
            if sweep == 1 and k == levels - 1:
                solved_ref[:, k, :] = carried
            else:
                state_ref[k] = carried
            unit[k] = unit_carried
        for k in range(levels - 2, -1, -1):
            above = upper[pl.ds(k, 1), :]
            carried = state_ref[k] + carried * above
            if sweep == 1:
                solved_ref[:, k, :] = carried
            else:
                state_ref[k] = carried
            unit[k] = unit[k] + unit[k + 1] * above
        for k in range(levels):
            unit_ref[sweep, pl.ds(k, 1), :] = unit[k]


def mix(tracers, diffusivity, column_depth):
    levels, fields, columns = tracers.shape
    vmem = pl.BlockSpec(memory_space=pltpu.VMEM)
    return pl.pallas_call(
        mix_kernel,
        out_shape=(jax.ShapeDtypeStruct((fields, levels, columns), F32),
                   jax.ShapeDtypeStruct((2, levels, columns), F32)),
        in_specs=[vmem] * 3,
        out_specs=(vmem, vmem),
        scratch_shapes=[pltpu.VMEM(tracers.shape, F32)] + [pltpu.VMEM((levels, columns), F32)] * 3,
        compiler_params=pltpu.CompilerParams(vmem_limit_bytes=24 << 20),
        cost_estimate=pl.CostEstimate(flops=12 * levels * fields * columns, transcendentals=0,
                                      bytes_accessed=6 * levels * fields * columns),
        name="mix",
    )(tracers, diffusivity, column_depth.reshape(1, columns))


def finish_kernel(scale, state_ref, unit_ref, rest_ref, near_ref, back_ref, total_ref, out_hbm,
                  surface, result, sems):
    fields, levels, columns = state_ref.shape
    eye = (lax.broadcasted_iota(jnp.int32, (ROWS, ROWS), 0)
           == lax.broadcasted_iota(jnp.int32, (ROWS, ROWS), 1))
    total = (total_ref[...] + total_in(near_ref[0]) + total_in(back_ref[0])) * scale
    spread = jnp.where(eye, jnp.broadcast_to(total, (ROWS, ROWS)), 0.0)
    fix = jnp.sum(spread, axis=1, keepdims=True)
    for o in range(2):
        surface[:, pl.ds(o * TILE, TILE)] = (rest_ref[o, 0] + near_ref[o].astype(F32)
                                             + back_ref[o].astype(F32)) + fix
    once = unit_ref[0]
    twice = unit_ref[1]
    copies = []
    for start in range(0, fields, FIELD_CHUNK):
        for f in range(start, start + FIELD_CHUNK):
            result[f] = (state_ref[f] + surface[pl.ds(f, 1), :] * twice
                         + surface[pl.ds(HALF + f, 1), :] * once)
        part = pl.ds(start, FIELD_CHUNK)
        copies.append(pltpu.make_async_copy(result.at[part], out_hbm.at[part],
                                            sems.at[start // FIELD_CHUNK]))
        copies[-1].start()
    for copy in copies:
        copy.wait()


def finish(state, unit, rest, near, back, total, scale):
    vmem = pl.BlockSpec(memory_space=pltpu.VMEM)
    fields, levels, columns = state.shape
    return pl.pallas_call(
        functools.partial(finish_kernel, scale),
        out_shape=jax.ShapeDtypeStruct(state.shape, F32),
        in_specs=[vmem] * 6,
        out_specs=pl.BlockSpec(memory_space=pltpu.HBM),
        scratch_shapes=[pltpu.VMEM((ROWS, columns), F32), pltpu.VMEM(state.shape, F32),
                        pltpu.SemaphoreType.DMA((fields // FIELD_CHUNK,))],
        compiler_params=pltpu.CompilerParams(vmem_limit_bytes=24 << 20),
        name="finish",
    )(state, unit, rest, near, back, total)


def shift(x, by, ring):
    return lax.ppermute(x, "blk", [(i, (i + by) % ring) for i in range(ring)])


def body(
    atm_flux,
    tile_bank,
    pair_count,
    pair_source,
    pair_tile,
    pair_target,
    tracers,
    diffusivity,
    column_depth,
):
    ring = lax.axis_size("blk")
    plane = lax.axis_size("sec") * lax.axis_size("grp")
    columns = tracers.shape[2]
    me = lax.axis_index("blk").astype(jnp.int32).reshape(1)
    right, left, keep, part = remap(pair_count, me, pair_source, pair_tile, pair_target, atm_flux,
                                    tile_bank, ring)
    right = shift(right, 1, ring)
    left = shift(left, -1, ring)
    column_depth, part = lax.optimization_barrier((column_depth, part))
    state, unit = mix(tracers, diffusivity, column_depth)
    part, unit = lax.optimization_barrier((part, unit))
    gathered = lax.all_to_all(jnp.broadcast_to(part[:1], (plane, ROWS)), ("sec", "grp"), 0, 0,
                              tiled=True)
    gathered, right = lax.optimization_barrier((gathered, right))
    own, near, back, far, other = combine(keep, right, left)
    group = ring // 4
    total = jnp.broadcast_to(jnp.sum(gathered, axis=0, keepdims=True), (group, ROWS))
    total = lax.all_to_all(total, "blk", 0, 0, tiled=True,
                           axis_index_groups=[[g * group + i for i in range(group)]
                                              for g in range(4)])
    near = shift(near, 2, ring)
    back = shift(back, -2, ring)
    far = shift(far, 4, ring)
    other = shift(other, -4, ring)
    total, near = lax.optimization_barrier((total, near))
    total = jnp.sum(total, axis=0, keepdims=True)
    outer, mirror, rest = gather(own, near, back, far, other, total)
    outer = shift(outer, 8, ring)
    mirror = shift(mirror, -8, ring)
    near, back = relay(rest, outer, mirror, total)
    near = shift(near, 8, ring)
    back = shift(back, -8, ring)
    result = finish(state, unit, rest, near, back, total, 1.0 / (columns * ring * plane))
    return jnp.transpose(result, (1, 0, 2))


def solution(mesh):
    placed = (
        P(None, None, ("sec", "grp", "blk")),
        P(),
        P(("sec", "grp", "blk")),
        P(("sec", "grp", "blk")),
        P(("sec", "grp", "blk")),
        P(("sec", "grp", "blk")),
        P(None, None, ("sec", "grp", "blk")),
        P(None, ("sec", "grp", "blk")),
        P(("sec", "grp", "blk")),
    )
    return jax.shard_map(
        body,
        mesh=mesh,
        in_specs=placed,
        out_specs=P(None, None, ("sec", "grp", "blk")),
        check_vma=False,
    )
```

```python
import functools

import jax
import jax.numpy as jnp
from jax import lax
from jax.experimental import pallas as pl
from jax.experimental.pallas import tpu as pltpu
from jax.sharding import PartitionSpec as P

F32 = jnp.float32
BF16 = jnp.bfloat16
HALF = 64
ROWS = 128
TILE = 128
UNROLL = 4
BANK_COPIES = 8
FIELD_CHUNK = 15
AHEAD = 13
PLUS = 10
MINUS = 11


def remap_kernel(count_ref, me_ref, source_hbm, tile_hbm, target_hbm, flux_ref, bank_hbm,
                 right_ref, left_ref, keep_ref, part_ref,
                 source_ref, tile_ref, target_ref, bank_ref, blocks, acc, list_sem, bank_sem):
    subs, fields, atm_rows = flux_ref.shape
    source_blocks = atm_rows // TILE
    slots = (acc.shape[0] - 1) // 2
    lists = [pltpu.make_async_copy(src, dst, list_sem.at[i]) for i, (src, dst) in enumerate(
        ((source_hbm, source_ref), (tile_hbm, tile_ref), (target_hbm, target_ref)))]
    span = bank_ref.shape[0] // BANK_COPIES
    loads = [pltpu.make_async_copy(bank_hbm.at[pl.ds(i * span, span)],
                                   bank_ref.at[pl.ds(i * span, span)], bank_sem.at[i])
             for i in range(BANK_COPIES)]
    for copy in lists + loads:
        copy.start()
    blocks[...] = jnp.zeros(blocks.shape, BF16)
    atm = jnp.zeros((ROWS, TILE), F32)
    for s in range(source_blocks):
        for sub in range(subs):
            blocks[s, pl.ds(sub * HALF, fields)] = flux_ref[sub, :, pl.ds(s * TILE, TILE)]
        atm = atm + blocks[s].astype(F32)
    acc[...] = jnp.zeros(acc.shape, F32)
    count = count_ref[0]
    me = me_ref[0]
    for copy in lists + loads:
        copy.wait()

    def slot_of(p):
        target = target_ref[p]
        half = target & 1
        owner = target >> 1
        away = (jnp.where(half == 0, owner - me, me - owner) + AHEAD) & (slots - 1)
        return jnp.where(p < count, half * slots + away, 2 * slots)

    def group(g, carry):
        terms = []
        for j in range(UNROLL):
            p = g * UNROLL + j
            terms.append(jnp.dot(blocks[source_ref[p]], bank_ref[tile_ref[p]],
                                 preferred_element_type=F32))
        for j in range(UNROLL):
            place = slot_of(g * UNROLL + j)
            acc[place] = acc[place] + terms[j]
        return carry

    lax.fori_loop(0, (count + UNROLL - 1) // UNROLL, group, 0)

    ocean = jnp.zeros((ROWS, TILE), F32)
    for half in range(2):
        for away in range(slots):
            value = acc[half * slots + away].astype(BF16)
            ocean = ocean + value.astype(F32)
            place, digit = away // 3, away % 3
            if digit == 1:
                keep_ref[half, place] = value
            elif (digit == 2) == (half == 0):
                right_ref[place + (0 if half == 0 else PLUS)] = value
            else:
                left_ref[place + (0 if half == 0 else MINUS)] = value
    share = 2.0 * TILE / atm_rows
    part = atm * share - ocean
    part_ref[...] = lax.dot_general(jnp.ones((8, TILE), F32), part, (((1,), (1,)), ((), ())),
                                    precision=lax.Precision.HIGHEST, preferred_element_type=F32)


def remap(pair_count, me, pair_source, pair_tile, pair_target, flux, bank, slots):
    smem = pl.BlockSpec(memory_space=pltpu.SMEM)
    vmem = pl.BlockSpec(memory_space=pltpu.VMEM)
    hbm = pl.BlockSpec(memory_space=pltpu.HBM)
    source_blocks = flux.shape[2] // TILE
    return pl.pallas_call(
        remap_kernel,
        out_shape=(jax.ShapeDtypeStruct((PLUS + MINUS, ROWS, TILE), BF16),
                   jax.ShapeDtypeStruct((PLUS + MINUS, ROWS, TILE), BF16),
                   jax.ShapeDtypeStruct((2, MINUS, ROWS, TILE), BF16),
                   jax.ShapeDtypeStruct((8, ROWS), F32)),
        in_specs=[smem] * 2 + [hbm] * 3 + [vmem, hbm],
        out_specs=(vmem,) * 4,
        scratch_shapes=[pltpu.SMEM(pair_source.shape, jnp.int32)] * 3
        + [pltpu.VMEM(bank.shape, BF16),
           pltpu.VMEM((source_blocks, ROWS, TILE), BF16),
           pltpu.VMEM((2 * slots + 1, ROWS, TILE), F32),
           pltpu.SemaphoreType.DMA((3,)),
           pltpu.SemaphoreType.DMA((BANK_COPIES,))],
        compiler_params=pltpu.CompilerParams(vmem_limit_bytes=40 << 20),
        cost_estimate=pl.CostEstimate(flops=2 * 128 * 128 ** 3, transcendentals=0,
                                      bytes_accessed=8 << 20),
        name="remap",
    )(pair_count, me, *(pltpu.with_memory_space_constraint(x, pltpu.HBM)
                        for x in (pair_source, pair_tile, pair_target)), flux,
      pltpu.with_memory_space_constraint(bank, pltpu.HBM))


def combine_kernel(keep_ref, right_ref, left_ref, own_ref, near_ref, back_ref):
    for o in range(2):
        for place in range(MINUS):
            value = keep_ref[o, place].astype(F32)
            plus, minus = (right_ref, left_ref) if o == 0 else (left_ref, right_ref)
            if place < PLUS:
                value = value + plus[place + (0 if o == 0 else MINUS)].astype(F32)
            value = value + minus[place + (0 if o == 0 else PLUS)].astype(F32)
            code, digit = place // 3, place % 3
            if digit == 1:
                own_ref[o, code] = value
            elif (digit == 2) == (o == 0):
                near_ref[code + (0 if o == 0 else 3)] = value.astype(BF16)
            else:
                back_ref[code + (0 if o == 0 else 4)] = value.astype(BF16)


def combine(keep, right, left):
    vmem = pl.BlockSpec(memory_space=pltpu.VMEM)
    sent = jax.ShapeDtypeStruct((7, ROWS, TILE), BF16)
    return pl.pallas_call(
        combine_kernel,
        out_shape=(jax.ShapeDtypeStruct((2, 4, ROWS, TILE), F32), sent, sent),
        in_specs=[vmem] * 3,
        out_specs=(vmem,) * 3,
        compiler_params=pltpu.CompilerParams(vmem_limit_bytes=16 << 20),
        name="combine",
    )(keep, right, left)


def with_total(chunk, total):
    row = lax.broadcasted_iota(jnp.int32, chunk.shape, 0)
    for i in range(3):
        piece = total.astype(BF16).astype(F32)
        chunk = jnp.where(row == HALF - 4 + i, piece, chunk)
        total = total - piece
    return chunk.astype(BF16)


def total_in(chunk):
    rows = chunk.astype(F32)
    place = HALF - 4
    return rows[place:place + 1] + rows[place + 1:place + 2] + rows[place + 2:place + 3]


def gather_kernel(own_ref, near_ref, back_ref, window_ref, tail_ref,
                  rest_ref, plus_ref, minus_ref, far_ref, other_ref):
    for o in range(2):
        for code in range(4):
            value = own_ref[o, code]
            up, down = (near_ref, back_ref) if o == 0 else (back_ref, near_ref)
            if code < 3:
                value = value + up[code + (0 if o == 0 else 4)].astype(F32)
            value = value + down[code + (0 if o == 0 else 3)].astype(F32)
            if code == 1:
                rest_ref[o] = value
            elif code == 3 and o == 0:
                far_ref[...] = with_total(value, tail_ref[...])
            elif code == 3:
                other_ref[...] = value.astype(BF16)
            else:
                sent = with_total(value, window_ref[...]) if o == 0 else value.astype(BF16)
                if (code == 2) == (o == 0):
                    plus_ref[o] = sent
                else:
                    minus_ref[o] = sent


def gather(own, near, back, window, tail):
    vmem = pl.BlockSpec(memory_space=pltpu.VMEM)
    chunk = jax.ShapeDtypeStruct((ROWS, TILE), BF16)
    pair = jax.ShapeDtypeStruct((2, ROWS, TILE), BF16)
    return pl.pallas_call(
        gather_kernel,
        out_shape=(jax.ShapeDtypeStruct((2, ROWS, TILE), F32), pair, pair, chunk, chunk),
        in_specs=[vmem] * 5,
        out_specs=(vmem,) * 5,
        compiler_params=pltpu.CompilerParams(vmem_limit_bytes=16 << 20),
        name="gather",
    )(own, near, back, window, tail)


def mix_kernel(tracer_ref, diff_ref, depth_ref, solved_ref, unit_ref, state_ref, ahead, lower, upper):
    levels, fields, columns = tracer_ref.shape
    depth = depth_ref[...]
    zero = jnp.zeros((1, columns), F32)
    one = jnp.ones((1, columns), F32)

    def coupling(k):
        if k == 0 or k == levels:
            return zero
        return jnp.where(depth > k, diff_ref[pl.ds(k - 1, 1), :], zero)

    ratio = None
    for k in range(levels):
        a, b = coupling(k), coupling(k + 1)
        pivot = 1.0 + a + b
        if k > 0:
            pivot = pivot - a * ratio
        inverse = 1.0 / pivot
        ratio = b * inverse
        wet = jnp.where(depth > k, one, zero)
        ahead[pl.ds(k, 1), :] = wet * inverse
        lower[pl.ds(k, 1), :] = a * inverse
        upper[pl.ds(k, 1), :] = ratio
    unit = [jnp.where(depth > 0, one, zero)] + [zero] * (levels - 1)
    for sweep in range(2):
        carried = None
        unit_carried = None
        for k in range(levels):
            if sweep == 0:
                x = tracer_ref[k].astype(F32)
            else:
                x = state_ref[k]
            scale = ahead[pl.ds(k, 1), :]
            below = lower[pl.ds(k, 1), :]
            if k == 0:
                carried = x * scale
                unit_carried = unit[k] * scale
            else:
                carried = x * scale + carried * below
                unit_carried = unit[k] * scale + unit_carried * below
            if sweep == 1 and k == levels - 1:
                solved_ref[:, k, :] = carried
            else:
                state_ref[k] = carried
            unit[k] = unit_carried
        for k in range(levels - 2, -1, -1):
            above = upper[pl.ds(k, 1), :]
            carried = state_ref[k] + carried * above
            if sweep == 1:
                solved_ref[:, k, :] = carried
            else:
                state_ref[k] = carried
            unit[k] = unit[k] + unit[k + 1] * above
        for k in range(levels):
            unit_ref[sweep, pl.ds(k, 1), :] = unit[k]


def mix(tracers, diffusivity, column_depth):
    levels, fields, columns = tracers.shape
    vmem = pl.BlockSpec(memory_space=pltpu.VMEM)
    return pl.pallas_call(
        mix_kernel,
        out_shape=(jax.ShapeDtypeStruct((fields, levels, columns), F32),
                   jax.ShapeDtypeStruct((2, levels, columns), F32)),
        in_specs=[vmem] * 3,
        out_specs=(vmem, vmem),
        scratch_shapes=[pltpu.VMEM(tracers.shape, F32)] + [pltpu.VMEM((levels, columns), F32)] * 3,
        compiler_params=pltpu.CompilerParams(vmem_limit_bytes=24 << 20),
        cost_estimate=pl.CostEstimate(flops=12 * levels * fields * columns, transcendentals=0,
                                      bytes_accessed=6 * levels * fields * columns),
        name="mix",
    )(tracers, diffusivity, column_depth.reshape(1, columns))


def finish_kernel(scale, state_ref, unit_ref, rest_ref, plus_ref, minus_ref, far_ref, other_ref,
                  total_ref, out_hbm,
                  surface, result, sems):
    fields, levels, columns = state_ref.shape
    eye = (lax.broadcasted_iota(jnp.int32, (ROWS, ROWS), 0)
           == lax.broadcasted_iota(jnp.int32, (ROWS, ROWS), 1))
    total = (total_ref[...] + total_in(plus_ref[0]) + total_in(minus_ref[0])
             + total_in(far_ref[...])) * scale
    spread = jnp.where(eye, jnp.broadcast_to(total, (ROWS, ROWS)), 0.0)
    fix = jnp.sum(spread, axis=1, keepdims=True)
    for o in range(2):
        last = (far_ref, other_ref)[o]
        surface[:, pl.ds(o * TILE, TILE)] = (rest_ref[o] + plus_ref[o].astype(F32)
                                             + minus_ref[o].astype(F32)
                                             + last[...].astype(F32)) + fix
    once = unit_ref[0]
    twice = unit_ref[1]
    copies = []
    for start in range(0, fields, FIELD_CHUNK):
        for f in range(start, start + FIELD_CHUNK):
            result[f] = (state_ref[f] + surface[pl.ds(f, 1), :] * twice
                         + surface[pl.ds(HALF + f, 1), :] * once)
        part = pl.ds(start, FIELD_CHUNK)
        copies.append(pltpu.make_async_copy(result.at[part], out_hbm.at[part],
                                            sems.at[start // FIELD_CHUNK]))
        copies[-1].start()
    for copy in copies:
        copy.wait()


def finish(state, unit, rest, plus, minus, far, other, total, scale):
    vmem = pl.BlockSpec(memory_space=pltpu.VMEM)
    fields, levels, columns = state.shape
    return pl.pallas_call(
        functools.partial(finish_kernel, scale),
        out_shape=jax.ShapeDtypeStruct(state.shape, F32),
        in_specs=[vmem] * 8,
        out_specs=pl.BlockSpec(memory_space=pltpu.HBM),
        scratch_shapes=[pltpu.VMEM((ROWS, columns), F32), pltpu.VMEM(state.shape, F32),
                        pltpu.SemaphoreType.DMA((fields // FIELD_CHUNK,))],
        compiler_params=pltpu.CompilerParams(vmem_limit_bytes=24 << 20),
        name="finish",
    )(state, unit, rest, plus, minus, far, other, total)


def shift(x, by, ring):
    return lax.ppermute(x, "blk", [(i, (i + by) % ring) for i in range(ring)])


def body(
    atm_flux,
    tile_bank,
    pair_count,
    pair_source,
    pair_tile,
    pair_target,
    tracers,
    diffusivity,
    column_depth,
):
    ring = lax.axis_size("blk")
    plane = lax.axis_size("sec") * lax.axis_size("grp")
    columns = tracers.shape[2]
    me = lax.axis_index("blk").astype(jnp.int32).reshape(1)
    right, left, keep, part = remap(pair_count, me, pair_source, pair_tile, pair_target, atm_flux,
                                    tile_bank, ring)
    right = shift(right, 1, ring)
    left = shift(left, -1, ring)
    gathered = lax.all_to_all(jnp.broadcast_to(part[:1], (plane, ROWS)), ("sec", "grp"), 0, 0,
                              tiled=True)
    gathered, right = lax.optimization_barrier((gathered, right))
    own, near, back = combine(keep, right, left)
    near = shift(near, 3, ring)
    back = shift(back, -3, ring)
    gathered, own = lax.optimization_barrier((gathered, own))
    column_depth, own = lax.optimization_barrier((column_depth, own))
    state, unit = mix(tracers, diffusivity, column_depth)
    level = jnp.sum(gathered, axis=0, keepdims=True)
    before, after = shift(level, 1, ring), shift(level, -1, ring)
    three = level + before + after
    behind, beyond = shift(three, 3, ring), shift(three, -3, ring)
    window = three + behind + beyond
    tail = level + after + beyond
    window, tail, near, back = lax.optimization_barrier((window, tail, near, back))
    rest, plus, minus, far, other = gather(own, near, back, window, tail)
    far = shift(far, -14, ring)
    other = shift(other, 14, ring)
    plus = shift(plus, 9, ring)
    minus = shift(minus, -9, ring)
    result = finish(state, unit, rest, plus, minus, far, other, window,
                    1.0 / (columns * ring * plane))
    return jnp.transpose(result, (1, 0, 2))


def solution(mesh):
    placed = (
        P(None, None, ("sec", "grp", "blk")),
        P(),
        P(("sec", "grp", "blk")),
        P(("sec", "grp", "blk")),
        P(("sec", "grp", "blk")),
        P(("sec", "grp", "blk")),
        P(None, None, ("sec", "grp", "blk")),
        P(None, ("sec", "grp", "blk")),
        P(("sec", "grp", "blk")),
    )
    return jax.shard_map(
        body,
        mesh=mesh,
        in_specs=placed,
        out_specs=P(None, None, ("sec", "grp", "blk")),
        check_vma=False,
    )
```

```python
import functools

import jax
import jax.numpy as jnp
from jax import lax
from jax.experimental import pallas as pl
from jax.experimental.pallas import tpu as pltpu
from jax.sharding import PartitionSpec as P

F32 = jnp.float32
BF16 = jnp.bfloat16
HALF = 64
ROWS = 128
TILE = 128
UNROLL = 4
BANK_COPIES = 8
FIELD_CHUNK = 15
FAR_STEP = 11
MID_STEP = 4
AHEAD = FAR_STEP + MID_STEP + 1
PLUS = 8
MINUS = 9
TWO = 6


def remap_kernel(count_ref, me_ref, source_hbm, tile_hbm, target_hbm, flux_ref, bank_hbm,
                 right_ref, left_ref, ahead_ref, astern_ref, keep_ref, part_ref,
                 source_ref, tile_ref, target_ref, bank_ref, blocks, acc, list_sem, bank_sem):
    subs, fields, atm_rows = flux_ref.shape
    source_blocks = atm_rows // TILE
    slots = (acc.shape[0] - 1) // 2
    lists = [pltpu.make_async_copy(src, dst, list_sem.at[i]) for i, (src, dst) in enumerate(
        ((source_hbm, source_ref), (tile_hbm, tile_ref), (target_hbm, target_ref)))]
    span = bank_ref.shape[0] // BANK_COPIES
    loads = [pltpu.make_async_copy(bank_hbm.at[pl.ds(i * span, span)],
                                   bank_ref.at[pl.ds(i * span, span)], bank_sem.at[i])
             for i in range(BANK_COPIES)]
    for copy in lists + loads:
        copy.start()
    blocks[...] = jnp.zeros(blocks.shape, BF16)
    atm = jnp.zeros((ROWS, TILE), F32)
    for s in range(source_blocks):
        for sub in range(subs):
            blocks[s, pl.ds(sub * HALF, fields)] = flux_ref[sub, :, pl.ds(s * TILE, TILE)]
        atm = atm + blocks[s].astype(F32)
    acc[...] = jnp.zeros(acc.shape, F32)
    count = count_ref[0]
    me = me_ref[0]
    for copy in lists + loads:
        copy.wait()

    def slot_of(p):
        target = target_ref[p]
        half = target & 1
        owner = target >> 1
        away = (jnp.where(half == 0, owner - me, me - owner) + AHEAD) & (slots - 1)
        return jnp.where(p < count, half * slots + away, 2 * slots)

    def group(g, carry):
        terms = []
        for j in range(UNROLL):
            p = g * UNROLL + j
            terms.append(jnp.dot(blocks[source_ref[p]], bank_ref[tile_ref[p]],
                                 preferred_element_type=F32))
        for j in range(UNROLL):
            place = slot_of(g * UNROLL + j)
            acc[place] = acc[place] + terms[j]
        return carry

    lax.fori_loop(0, (count + UNROLL - 1) // UNROLL, group, 0)

    ocean = jnp.zeros((ROWS, TILE), F32)
    for half in range(2):
        for away in range(slots):
            value = acc[half * slots + away].astype(BF16)
            ocean = ocean + value.astype(F32)
            far, rest = divmod(away, FAR_STEP)
            mid, digit = divmod(rest, MID_STEP)
            place = 3 * far + mid
            if digit == 1:
                keep_ref[half, place] = value
            elif digit == 3:
                (ahead_ref, astern_ref)[half][2 * far + mid] = value
            elif (digit == 2) == (half == 0):
                right_ref[place + (0 if half == 0 else PLUS)] = value
            else:
                left_ref[place + (0 if half == 0 else MINUS)] = value
    share = 2.0 * TILE / atm_rows
    part = atm * share - ocean
    part_ref[...] = lax.dot_general(jnp.ones((8, TILE), F32), part, (((1,), (1,)), ((), ())),
                                    precision=lax.Precision.HIGHEST, preferred_element_type=F32)


def remap(pair_count, me, pair_source, pair_tile, pair_target, flux, bank, slots):
    smem = pl.BlockSpec(memory_space=pltpu.SMEM)
    vmem = pl.BlockSpec(memory_space=pltpu.VMEM)
    hbm = pl.BlockSpec(memory_space=pltpu.HBM)
    source_blocks = flux.shape[2] // TILE
    return pl.pallas_call(
        remap_kernel,
        out_shape=(jax.ShapeDtypeStruct((PLUS + MINUS, ROWS, TILE), BF16),
                   jax.ShapeDtypeStruct((PLUS + MINUS, ROWS, TILE), BF16),
                   jax.ShapeDtypeStruct((TWO, ROWS, TILE), BF16),
                   jax.ShapeDtypeStruct((TWO, ROWS, TILE), BF16),
                   jax.ShapeDtypeStruct((2, MINUS, ROWS, TILE), BF16),
                   jax.ShapeDtypeStruct((8, ROWS), F32)),
        in_specs=[smem] * 2 + [hbm] * 3 + [vmem, hbm],
        out_specs=(vmem,) * 6,
        scratch_shapes=[pltpu.SMEM(pair_source.shape, jnp.int32)] * 3
        + [pltpu.VMEM(bank.shape, BF16),
           pltpu.VMEM((source_blocks, ROWS, TILE), BF16),
           pltpu.VMEM((2 * slots + 1, ROWS, TILE), F32),
           pltpu.SemaphoreType.DMA((3,)),
           pltpu.SemaphoreType.DMA((BANK_COPIES,))],
        compiler_params=pltpu.CompilerParams(vmem_limit_bytes=40 << 20),
        cost_estimate=pl.CostEstimate(flops=2 * 128 * 128 ** 3, transcendentals=0,
                                      bytes_accessed=8 << 20),
        name="remap",
    )(pair_count, me, *(pltpu.with_memory_space_constraint(x, pltpu.HBM)
                        for x in (pair_source, pair_tile, pair_target)), flux,
      pltpu.with_memory_space_constraint(bank, pltpu.HBM))


def combine_kernel(keep_ref, right_ref, left_ref, ahead_ref, astern_ref,
                   own_ref, near_ref, back_ref):
    for o in range(2):
        plus, minus = (right_ref, left_ref) if o == 0 else (left_ref, right_ref)
        for place in range(MINUS):
            far, mid = divmod(place, 3)
            value = keep_ref[o, place].astype(F32)
            if place < PLUS:
                value = value + plus[place + (0 if o == 0 else MINUS)].astype(F32)
            value = value + minus[place + (0 if o == 0 else PLUS)].astype(F32)
            if mid < 2:
                value = value + (ahead_ref, astern_ref)[o][2 * far + mid].astype(F32)
            if mid == 1:
                own_ref[o, far] = value
            elif (mid == 2) == (o == 0):
                near_ref[far + 3 * o] = value.astype(BF16)
            else:
                back_ref[far + 3 * o] = value.astype(BF16)


def combine(keep, right, left, ahead, astern):
    vmem = pl.BlockSpec(memory_space=pltpu.VMEM)
    sent = jax.ShapeDtypeStruct((6, ROWS, TILE), BF16)
    return pl.pallas_call(
        combine_kernel,
        out_shape=(jax.ShapeDtypeStruct((2, 3, ROWS, TILE), F32), sent, sent),
        in_specs=[vmem] * 5,
        out_specs=(vmem,) * 3,
        compiler_params=pltpu.CompilerParams(vmem_limit_bytes=16 << 20),
        name="combine",
    )(keep, right, left, ahead, astern)


def with_total(chunk, total):
    row = lax.broadcasted_iota(jnp.int32, chunk.shape, 0)
    for i in range(3):
        piece = total.astype(BF16).astype(F32)
        chunk = jnp.where(row == HALF - 4 + i, piece, chunk)
        total = total - piece
    return chunk.astype(BF16)


def total_in(chunk):
    rows = chunk.astype(F32)
    place = HALF - 4
    return rows[place:place + 1] + rows[place + 1:place + 2] + rows[place + 2:place + 3]


def gather_kernel(own_ref, near_ref, back_ref, total_ref, rest_ref, plus_ref, minus_ref):
    for o in range(2):
        for far in range(3):
            value = (own_ref[o, far] + near_ref[far + 3 * o].astype(F32)
                     + back_ref[far + 3 * o].astype(F32))
            if far == 1:
                rest_ref[o] = value
                continue
            sent = with_total(value, total_ref[...]) if o == 0 else value.astype(BF16)
            if (far == 2) == (o == 0):
                plus_ref[o] = sent
            else:
                minus_ref[o] = sent


def gather(own, near, back, total):
    vmem = pl.BlockSpec(memory_space=pltpu.VMEM)
    pair = jax.ShapeDtypeStruct((2, ROWS, TILE), BF16)
    return pl.pallas_call(
        gather_kernel,
        out_shape=(jax.ShapeDtypeStruct((2, ROWS, TILE), F32), pair, pair),
        in_specs=[vmem] * 4,
        out_specs=(vmem,) * 3,
        compiler_params=pltpu.CompilerParams(vmem_limit_bytes=16 << 20),
        name="gather",
    )(own, near, back, total)


def mix_kernel(tracer_ref, diff_ref, depth_ref, solved_ref, unit_ref, state_ref, ahead, lower, upper):
    levels, fields, columns = tracer_ref.shape
    depth = depth_ref[...]
    zero = jnp.zeros((1, columns), F32)
    one = jnp.ones((1, columns), F32)

    def coupling(k):
        if k == 0 or k == levels:
            return zero
        return jnp.where(depth > k, diff_ref[pl.ds(k - 1, 1), :], zero)

    ratio = None
    for k in range(levels):
        a, b = coupling(k), coupling(k + 1)
        pivot = 1.0 + a + b
        if k > 0:
            pivot = pivot - a * ratio
        inverse = 1.0 / pivot
        ratio = b * inverse
        wet = jnp.where(depth > k, one, zero)
        ahead[pl.ds(k, 1), :] = wet * inverse
        lower[pl.ds(k, 1), :] = a * inverse
        upper[pl.ds(k, 1), :] = ratio
    unit = [jnp.where(depth > 0, one, zero)] + [zero] * (levels - 1)
    for sweep in range(2):
        carried = None
        unit_carried = None
        for k in range(levels):
            if sweep == 0:
                x = tracer_ref[k].astype(F32)
            else:
                x = state_ref[k]
            scale = ahead[pl.ds(k, 1), :]
            below = lower[pl.ds(k, 1), :]
            if k == 0:
                carried = x * scale
                unit_carried = unit[k] * scale
            else:
                carried = x * scale + carried * below
                unit_carried = unit[k] * scale + unit_carried * below
            if sweep == 1 and k == levels - 1:
                solved_ref[:, k, :] = carried
            else:
                state_ref[k] = carried
            unit[k] = unit_carried
        for k in range(levels - 2, -1, -1):
            above = upper[pl.ds(k, 1), :]
            carried = state_ref[k] + carried * above
            if sweep == 1:
                solved_ref[:, k, :] = carried
            else:
                state_ref[k] = carried
            unit[k] = unit[k] + unit[k + 1] * above
        for k in range(levels):
            unit_ref[sweep, pl.ds(k, 1), :] = unit[k]


def mix(tracers, diffusivity, column_depth):
    levels, fields, columns = tracers.shape
    vmem = pl.BlockSpec(memory_space=pltpu.VMEM)
    return pl.pallas_call(
        mix_kernel,
        out_shape=(jax.ShapeDtypeStruct((fields, levels, columns), F32),
                   jax.ShapeDtypeStruct((2, levels, columns), F32)),
        in_specs=[vmem] * 3,
        out_specs=(vmem, vmem),
        scratch_shapes=[pltpu.VMEM(tracers.shape, F32)] + [pltpu.VMEM((levels, columns), F32)] * 3,
        compiler_params=pltpu.CompilerParams(vmem_limit_bytes=24 << 20),
        cost_estimate=pl.CostEstimate(flops=12 * levels * fields * columns, transcendentals=0,
                                      bytes_accessed=6 * levels * fields * columns),
        name="mix",
    )(tracers, diffusivity, column_depth.reshape(1, columns))


def finish_kernel(scale, ring, me_ref, state_ref, unit_ref, rest_ref, plus_ref, minus_ref,
                  total_ref, out_hbm,
                  surface, result, sems):
    fields, levels, columns = state_ref.shape
    eye = (lax.broadcasted_iota(jnp.int32, (ROWS, ROWS), 0)
           == lax.broadcasted_iota(jnp.int32, (ROWS, ROWS), 1))
    me = me_ref[0]
    half = ring // 2
    crossed = ((me - FAR_STEP) & (ring - 1)) // half != me // half
    total = (total_ref[...] + jnp.where(crossed, total_in(plus_ref[0]),
                                        total_in(minus_ref[0]))) * scale
    spread = jnp.where(eye, jnp.broadcast_to(total, (ROWS, ROWS)), 0.0)
    fix = jnp.sum(spread, axis=1, keepdims=True)
    for o in range(2):
        surface[:, pl.ds(o * TILE, TILE)] = (rest_ref[o] + plus_ref[o].astype(F32)
                                             + minus_ref[o].astype(F32)) + fix
    once = unit_ref[0]
    twice = unit_ref[1]
    copies = []
    for start in range(0, fields, FIELD_CHUNK):
        for f in range(start, start + FIELD_CHUNK):
            result[f] = (state_ref[f] + surface[pl.ds(f, 1), :] * twice
                         + surface[pl.ds(HALF + f, 1), :] * once)
        part = pl.ds(start, FIELD_CHUNK)
        copies.append(pltpu.make_async_copy(result.at[part], out_hbm.at[part],
                                            sems.at[start // FIELD_CHUNK]))
        copies[-1].start()
    for copy in copies:
        copy.wait()


def finish(me, state, unit, rest, plus, minus, total, scale, ring):
    vmem = pl.BlockSpec(memory_space=pltpu.VMEM)
    fields, levels, columns = state.shape
    return pl.pallas_call(
        functools.partial(finish_kernel, scale, ring),
        out_shape=jax.ShapeDtypeStruct(state.shape, F32),
        in_specs=[pl.BlockSpec(memory_space=pltpu.SMEM)] + [vmem] * 6,
        out_specs=pl.BlockSpec(memory_space=pltpu.HBM),
        scratch_shapes=[pltpu.VMEM((ROWS, columns), F32), pltpu.VMEM(state.shape, F32),
                        pltpu.SemaphoreType.DMA((fields // FIELD_CHUNK,))],
        compiler_params=pltpu.CompilerParams(vmem_limit_bytes=24 << 20),
        name="finish",
    )(me, state, unit, rest, plus, minus, total)


def shift(x, by, ring):
    return lax.ppermute(x, "blk", [(i, (i + by) % ring) for i in range(ring)])


def body(
    atm_flux,
    tile_bank,
    pair_count,
    pair_source,
    pair_tile,
    pair_target,
    tracers,
    diffusivity,
    column_depth,
):
    ring = lax.axis_size("blk")
    plane = lax.axis_size("sec") * lax.axis_size("grp")
    columns = tracers.shape[2]
    me = lax.axis_index("blk").astype(jnp.int32).reshape(1)
    right, left, ahead, astern, keep, part = remap(
        pair_count, me, pair_source, pair_tile, pair_target, atm_flux, tile_bank, ring)
    ahead = shift(ahead, 2, ring)
    astern = shift(astern, -2, ring)
    right = shift(right, 1, ring)
    left = shift(left, -1, ring)
    gathered = lax.all_to_all(jnp.broadcast_to(part[:1], (plane, ROWS)), ("sec", "grp"), 0, 0,
                              tiled=True)
    gathered, right = lax.optimization_barrier((gathered, right))
    own, near, back = combine(keep, right, left, ahead, astern)
    near = shift(near, MID_STEP, ring)
    back = shift(back, -MID_STEP, ring)
    gathered, column_depth, own = lax.optimization_barrier((gathered, column_depth, own))
    state, unit = mix(tracers, diffusivity, column_depth)
    group = ring // 2
    total = jnp.broadcast_to(jnp.sum(gathered, axis=0, keepdims=True), (group, ROWS))
    total = lax.all_to_all(total, "blk", 0, 0, tiled=True,
                           axis_index_groups=[list(range(group)), list(range(group, ring))])
    total, near = lax.optimization_barrier((total, near))
    total = jnp.sum(total, axis=0, keepdims=True)
    rest, plus, minus = gather(own, near, back, total)
    plus = shift(plus, FAR_STEP, ring)
    minus = shift(minus, -FAR_STEP, ring)
    result = finish(me, state, unit, rest, plus, minus, total, 1.0 / (columns * ring * plane), ring)
    return jnp.transpose(result, (1, 0, 2))


def solution(mesh):
    placed = (
        P(None, None, ("sec", "grp", "blk")),
        P(),
        P(("sec", "grp", "blk")),
        P(("sec", "grp", "blk")),
        P(("sec", "grp", "blk")),
        P(("sec", "grp", "blk")),
        P(None, None, ("sec", "grp", "blk")),
        P(None, ("sec", "grp", "blk")),
        P(("sec", "grp", "blk")),
    )
    return jax.shard_map(
        body,
        mesh=mesh,
        in_specs=placed,
        out_specs=P(None, None, ("sec", "grp", "blk")),
        check_vma=False,
    )
```

```python
import functools

import jax
import jax.numpy as jnp
from jax import lax
from jax.experimental import pallas as pl
from jax.experimental.pallas import tpu as pltpu
from jax.sharding import PartitionSpec as P

F32 = jnp.float32
BF16 = jnp.bfloat16
ROWS = 120
FINAL_ROWS = 128
TILE = 128
UNROLL = 8
BANK_COPIES = 8
FIELD_CHUNK = 15
FAR_STEP = 11
MID_STEP = 4
AHEAD = FAR_STEP + MID_STEP + 1
PLUS = 8
MINUS = 9
TWO = 6


def remap_kernel(count_ref, me_ref, source_hbm, tile_hbm, target_hbm, flux_ref, bank_hbm,
                 right_ref, left_ref, ahead_ref, astern_ref, keep_ref, part_ref,
                 source_ref, tile_ref, target_ref, bank_ref, blocks, acc, list_sem, bank_sem):
    subs, fields, atm_rows = flux_ref.shape
    source_blocks = atm_rows // TILE
    slots = (acc.shape[0] - 1) // 2
    lists = [pltpu.make_async_copy(src, dst, list_sem.at[i]) for i, (src, dst) in enumerate(
        ((source_hbm, source_ref), (tile_hbm, tile_ref), (target_hbm, target_ref)))]
    span = bank_ref.shape[0] // BANK_COPIES
    loads = [pltpu.make_async_copy(bank_hbm.at[pl.ds(i * span, span)],
                                   bank_ref.at[pl.ds(i * span, span)], bank_sem.at[i])
             for i in range(BANK_COPIES)]
    for copy in lists + loads:
        copy.start()
    blocks[...] = jnp.zeros(blocks.shape, BF16)
    atm = jnp.zeros((ROWS, TILE), F32)
    for s in range(source_blocks):
        for sub in range(subs):
            blocks[s, pl.ds(sub * fields, fields)] = flux_ref[sub, :, pl.ds(s * TILE, TILE)]
        atm = atm + blocks[s].astype(F32)
    acc[...] = jnp.zeros(acc.shape, F32)
    count = count_ref[0]
    me = me_ref[0]
    for copy in lists + loads:
        copy.wait()

    def slot_of(p):
        target = target_ref[p]
        half = target & 1
        owner = target >> 1
        away = (jnp.where(half == 0, owner - me, me - owner) + AHEAD) & (slots - 1)
        return jnp.where(p < count, half * slots + away, 2 * slots)

    def group(g, carry):
        terms = []
        for j in range(UNROLL):
            p = g * UNROLL + j
            terms.append(jnp.dot(blocks[source_ref[p]], bank_ref[tile_ref[p]],
                                 preferred_element_type=F32))
        for j in range(UNROLL):
            place = slot_of(g * UNROLL + j)
            acc[place] = acc[place] + terms[j]
        return carry

    lax.fori_loop(0, (count + UNROLL - 1) // UNROLL, group, 0)

    ocean = jnp.zeros((ROWS, TILE), F32)
    for half in range(2):
        for away in range(slots):
            value = acc[half * slots + away].astype(BF16)
            ocean = ocean + value.astype(F32)
            far, rest = divmod(away, FAR_STEP)
            mid, digit = divmod(rest, MID_STEP)
            place = 3 * far + mid
            if digit == 1:
                keep_ref[half, place] = value
            elif digit == 3:
                (ahead_ref, astern_ref)[half][2 * far + mid] = value
            elif (digit == 2) == (half == 0):
                right_ref[place + (0 if half == 0 else PLUS)] = value
            else:
                left_ref[place + (0 if half == 0 else MINUS)] = value
    share = 2.0 * TILE / atm_rows
    part = jnp.concatenate([atm * share - ocean, jnp.zeros((TILE - ROWS, TILE), F32)], axis=0)
    part_ref[...] = lax.dot_general(jnp.ones((8, TILE), F32), part, (((1,), (1,)), ((), ())),
                                    precision=lax.Precision.HIGHEST, preferred_element_type=F32)


def remap(pair_count, me, pair_source, pair_tile, pair_target, flux, bank, slots):
    smem = pl.BlockSpec(memory_space=pltpu.SMEM)
    vmem = pl.BlockSpec(memory_space=pltpu.VMEM)
    hbm = pl.BlockSpec(memory_space=pltpu.HBM)
    source_blocks = flux.shape[2] // TILE
    return pl.pallas_call(
        remap_kernel,
        out_shape=(jax.ShapeDtypeStruct((PLUS + MINUS, ROWS, TILE), BF16),
                   jax.ShapeDtypeStruct((PLUS + MINUS, ROWS, TILE), BF16),
                   jax.ShapeDtypeStruct((TWO, ROWS, TILE), BF16),
                   jax.ShapeDtypeStruct((TWO, ROWS, TILE), BF16),
                   jax.ShapeDtypeStruct((2, MINUS, ROWS, TILE), BF16),
                   jax.ShapeDtypeStruct((8, TILE), F32)),
        in_specs=[smem] * 2 + [hbm] * 3 + [vmem, hbm],
        out_specs=(vmem,) * 6,
        scratch_shapes=[pltpu.SMEM(pair_source.shape, jnp.int32)] * 3
        + [pltpu.VMEM(bank.shape, BF16),
           pltpu.VMEM((source_blocks, ROWS, TILE), BF16),
           pltpu.VMEM((2 * slots + 1, ROWS, TILE), F32),
           pltpu.SemaphoreType.DMA((3,)),
           pltpu.SemaphoreType.DMA((BANK_COPIES,))],
        compiler_params=pltpu.CompilerParams(vmem_limit_bytes=40 << 20),
        cost_estimate=pl.CostEstimate(flops=2 * 128 * 128 ** 3, transcendentals=0,
                                      bytes_accessed=8 << 20),
        name="remap",
    )(pair_count, me, *(pltpu.with_memory_space_constraint(x, pltpu.HBM)
                        for x in (pair_source, pair_tile, pair_target)), flux,
      pltpu.with_memory_space_constraint(bank, pltpu.HBM))


def combine_kernel(keep_ref, right_ref, left_ref, ahead_ref, astern_ref,
                   own_ref, near_ref, back_ref):
    for o in range(2):
        plus, minus = (right_ref, left_ref) if o == 0 else (left_ref, right_ref)
        for place in range(MINUS):
            far, mid = divmod(place, 3)
            value = keep_ref[o, place].astype(F32)
            if place < PLUS:
                value = value + plus[place + (0 if o == 0 else MINUS)].astype(F32)
            value = value + minus[place + (0 if o == 0 else PLUS)].astype(F32)
            if mid < 2:
                value = value + (ahead_ref, astern_ref)[o][2 * far + mid].astype(F32)
            if mid == 1:
                own_ref[o, far] = value
            elif (mid == 2) == (o == 0):
                near_ref[far + 3 * o] = value.astype(BF16)
            else:
                back_ref[far + 3 * o] = value.astype(BF16)


def combine(keep, right, left, ahead, astern):
    vmem = pl.BlockSpec(memory_space=pltpu.VMEM)
    sent = jax.ShapeDtypeStruct((6, ROWS, TILE), BF16)
    return pl.pallas_call(
        combine_kernel,
        out_shape=(jax.ShapeDtypeStruct((2, 3, ROWS, TILE), F32), sent, sent),
        in_specs=[vmem] * 5,
        out_specs=(vmem,) * 3,
        compiler_params=pltpu.CompilerParams(vmem_limit_bytes=16 << 20),
        name="combine",
    )(keep, right, left, ahead, astern)


def with_total(chunk, total):
    row = lax.broadcasted_iota(jnp.int32, (FINAL_ROWS - ROWS, TILE), 0)
    tail = jnp.zeros((FINAL_ROWS - ROWS, TILE), F32)
    for i in range(3):
        piece = total.astype(BF16).astype(F32)
        tail = jnp.where(row == i, piece, tail)
        total = total - piece
    return jnp.concatenate([chunk, tail], axis=0).astype(BF16)


def total_in(chunk):
    rows = chunk.astype(F32)
    return rows[ROWS:ROWS + 1] + rows[ROWS + 1:ROWS + 2] + rows[ROWS + 2:ROWS + 3]


def gather_kernel(own_ref, near_ref, back_ref, total_ref, rest_ref, plus_ref, minus_ref):
    for o in range(2):
        for far in range(3):
            value = (own_ref[o, far] + near_ref[far + 3 * o].astype(F32)
                     + back_ref[far + 3 * o].astype(F32))
            if far == 1:
                rest_ref[o] = value
                continue
            sent = with_total(value, total_ref[...])
            if (far == 2) == (o == 0):
                plus_ref[o] = sent
            else:
                minus_ref[o] = sent


def gather(own, near, back, total):
    vmem = pl.BlockSpec(memory_space=pltpu.VMEM)
    pair = jax.ShapeDtypeStruct((2, FINAL_ROWS, TILE), BF16)
    return pl.pallas_call(
        gather_kernel,
        out_shape=(jax.ShapeDtypeStruct((2, ROWS, TILE), F32), pair, pair),
        in_specs=[vmem] * 4,
        out_specs=(vmem,) * 3,
        compiler_params=pltpu.CompilerParams(vmem_limit_bytes=16 << 20),
        name="gather",
    )(own, near, back, total)


def mix_kernel(tracer_ref, diff_ref, depth_ref, solved_ref, unit_ref, state_ref, ahead, lower, upper):
    levels, fields, columns = tracer_ref.shape
    depth = depth_ref[...]
    zero = jnp.zeros((1, columns), F32)
    one = jnp.ones((1, columns), F32)

    def coupling(k):
        if k == 0 or k == levels:
            return zero
        return jnp.where(depth > k, diff_ref[pl.ds(k - 1, 1), :], zero)

    ratio = None
    for k in range(levels):
        a, b = coupling(k), coupling(k + 1)
        pivot = 1.0 + a + b
        if k > 0:
            pivot = pivot - a * ratio
        inverse = 1.0 / pivot
        ratio = b * inverse
        wet = jnp.where(depth > k, one, zero)
        ahead[pl.ds(k, 1), :] = wet * inverse
        lower[pl.ds(k, 1), :] = a * inverse
        upper[pl.ds(k, 1), :] = ratio
    unit = [jnp.where(depth > 0, one, zero)] + [zero] * (levels - 1)
    for sweep in range(2):
        carried = None
        unit_carried = None
        for k in range(levels):
            if sweep == 0:
                x = tracer_ref[k].astype(F32)
            else:
                x = state_ref[k]
            scale = ahead[pl.ds(k, 1), :]
            below = lower[pl.ds(k, 1), :]
            if k == 0:
                carried = x * scale
                unit_carried = unit[k] * scale
            else:
                carried = x * scale + carried * below
                unit_carried = unit[k] * scale + unit_carried * below
            if sweep == 1 and k == levels - 1:
                solved_ref[:, k, :] = carried
            else:
                state_ref[k] = carried
            unit[k] = unit_carried
        for k in range(levels - 2, -1, -1):
            above = upper[pl.ds(k, 1), :]
            carried = state_ref[k] + carried * above
            if sweep == 1:
                solved_ref[:, k, :] = carried
            else:
                state_ref[k] = carried
            unit[k] = unit[k] + unit[k + 1] * above
        for k in range(levels):
            unit_ref[sweep, pl.ds(k, 1), :] = unit[k]


def mix(tracers, diffusivity, column_depth):
    levels, fields, columns = tracers.shape
    vmem = pl.BlockSpec(memory_space=pltpu.VMEM)
    return pl.pallas_call(
        mix_kernel,
        out_shape=(jax.ShapeDtypeStruct((fields, levels, columns), F32),
                   jax.ShapeDtypeStruct((2, levels, columns), F32)),
        in_specs=[vmem] * 3,
        out_specs=(vmem, vmem),
        scratch_shapes=[pltpu.VMEM(tracers.shape, F32)] + [pltpu.VMEM((levels, columns), F32)] * 3,
        compiler_params=pltpu.CompilerParams(vmem_limit_bytes=24 << 20),
        cost_estimate=pl.CostEstimate(flops=12 * levels * fields * columns, transcendentals=0,
                                      bytes_accessed=6 * levels * fields * columns),
        name="mix",
    )(tracers, diffusivity, column_depth.reshape(1, columns))


def finish_kernel(scale, ring, me_ref, state_ref, unit_ref, rest_ref, plus_ref, minus_ref,
                  total_ref, out_hbm,
                  surface, result, sems):
    fields, levels, columns = state_ref.shape
    eye = (lax.broadcasted_iota(jnp.int32, (ROWS, TILE), 0)
           == lax.broadcasted_iota(jnp.int32, (ROWS, TILE), 1))
    me = me_ref[0]
    half = ring // 2
    crossed = ((me - FAR_STEP) & (ring - 1)) // half != me // half
    total = (total_ref[...] + jnp.where(crossed, total_in(plus_ref[0]),
                                        total_in(minus_ref[0]))) * scale
    spread = jnp.where(eye, jnp.broadcast_to(total, (ROWS, TILE)), 0.0)
    fix = jnp.sum(spread, axis=1, keepdims=True)
    for o in range(2):
        surface[:, pl.ds(o * TILE, TILE)] = (rest_ref[o] + plus_ref[o].astype(F32)[:ROWS]
                                             + minus_ref[o].astype(F32)[:ROWS]) + fix
    once = unit_ref[0]
    twice = unit_ref[1]
    copies = []
    for start in range(0, fields, FIELD_CHUNK):
        for f in range(start, start + FIELD_CHUNK):
            result[f] = (state_ref[f] + surface[pl.ds(f, 1), :] * twice
                         + surface[pl.ds(fields + f, 1), :] * once)
        part = pl.ds(start, FIELD_CHUNK)
        copies.append(pltpu.make_async_copy(result.at[part], out_hbm.at[part],
                                            sems.at[start // FIELD_CHUNK]))
        copies[-1].start()
    for copy in copies:
        copy.wait()


def finish(me, state, unit, rest, plus, minus, total, scale, ring):
    vmem = pl.BlockSpec(memory_space=pltpu.VMEM)
    fields, levels, columns = state.shape
    return pl.pallas_call(
        functools.partial(finish_kernel, scale, ring),
        out_shape=jax.ShapeDtypeStruct(state.shape, F32),
        in_specs=[pl.BlockSpec(memory_space=pltpu.SMEM)] + [vmem] * 6,
        out_specs=pl.BlockSpec(memory_space=pltpu.HBM),
        scratch_shapes=[pltpu.VMEM((ROWS, columns), F32), pltpu.VMEM(state.shape, F32),
                        pltpu.SemaphoreType.DMA((fields // FIELD_CHUNK,))],
        compiler_params=pltpu.CompilerParams(vmem_limit_bytes=24 << 20),
        name="finish",
    )(me, state, unit, rest, plus, minus, total)


def shift(x, by, ring):
    return lax.ppermute(x, "blk", [(i, (i + by) % ring) for i in range(ring)])


def body(
    atm_flux,
    tile_bank,
    pair_count,
    pair_source,
    pair_tile,
    pair_target,
    tracers,
    diffusivity,
    column_depth,
):
    ring = lax.axis_size("blk")
    plane = lax.axis_size("sec") * lax.axis_size("grp")
    columns = tracers.shape[2]
    me = lax.axis_index("blk").astype(jnp.int32).reshape(1)
    right, left, ahead, astern, keep, part = remap(
        pair_count, me, pair_source, pair_tile, pair_target, atm_flux, tile_bank, ring)
    ahead = shift(ahead, 2, ring)
    astern = shift(astern, -2, ring)
    right = shift(right, 1, ring)
    left = shift(left, -1, ring)
    gathered = lax.all_to_all(jnp.broadcast_to(part[:1], (plane, TILE)), ("sec", "grp"), 0, 0,
                              tiled=True)
    gathered, right = lax.optimization_barrier((gathered, right))
    own, near, back = combine(keep, right, left, ahead, astern)
    near = shift(near, MID_STEP, ring)
    back = shift(back, -MID_STEP, ring)
    gathered, column_depth, own = lax.optimization_barrier((gathered, column_depth, own))
    state, unit = mix(tracers, diffusivity, column_depth)
    group = ring // 2
    total = jnp.broadcast_to(jnp.sum(gathered, axis=0, keepdims=True), (group, TILE))
    total = lax.all_to_all(total, "blk", 0, 0, tiled=True,
                           axis_index_groups=[list(range(group)), list(range(group, ring))])
    total, near = lax.optimization_barrier((total, near))
    total = jnp.sum(total, axis=0, keepdims=True)
    rest, plus, minus = gather(own, near, back, total)
    plus = shift(plus, FAR_STEP, ring)
    minus = shift(minus, -FAR_STEP, ring)
    result = finish(me, state, unit, rest, plus, minus, total, 1.0 / (columns * ring * plane), ring)
    return jnp.transpose(result, (1, 0, 2))


def solution(mesh):
    placed = (
        P(None, None, ("sec", "grp", "blk")),
        P(),
        P(("sec", "grp", "blk")),
        P(("sec", "grp", "blk")),
        P(("sec", "grp", "blk")),
        P(("sec", "grp", "blk")),
        P(None, None, ("sec", "grp", "blk")),
        P(None, ("sec", "grp", "blk")),
        P(("sec", "grp", "blk")),
    )
    return jax.shard_map(
        body,
        mesh=mesh,
        in_specs=placed,
        out_specs=P(None, None, ("sec", "grp", "blk")),
        check_vma=False,
    )
```

```python
import functools

import jax
import jax.numpy as jnp
from jax import lax
from jax.experimental import pallas as pl
from jax.experimental.pallas import tpu as pltpu
from jax.sharding import PartitionSpec as P

F32 = jnp.float32
BF16 = jnp.bfloat16
ROWS = 120
TILE = 128
UNROLL = 8
BANK_COPIES = 8
FIELD_CHUNK = 15
FAR_STEP = 11
MID_STEP = 4
AHEAD = FAR_STEP + MID_STEP + 1
PLUS = 8
MINUS = 9
TWO = 6


def remap_kernel(count_ref, me_ref, source_hbm, tile_hbm, target_hbm, flux_ref, bank_hbm,
                 right_ref, left_ref, ahead_ref, astern_ref, keep_ref, part_ref,
                 source_ref, tile_ref, target_ref, bank_ref, blocks, acc, list_sem, bank_sem):
    subs, fields, atm_rows = flux_ref.shape
    source_blocks = atm_rows // TILE
    slots = (acc.shape[0] - 1) // 2
    lists = [pltpu.make_async_copy(src, dst, list_sem.at[i]) for i, (src, dst) in enumerate(
        ((source_hbm, source_ref), (tile_hbm, tile_ref), (target_hbm, target_ref)))]
    span = bank_ref.shape[0] // BANK_COPIES
    loads = [pltpu.make_async_copy(bank_hbm.at[pl.ds(i * span, span)],
                                   bank_ref.at[pl.ds(i * span, span)], bank_sem.at[i])
             for i in range(BANK_COPIES)]
    for copy in lists + loads:
        copy.start()
    blocks[...] = jnp.zeros(blocks.shape, BF16)
    atm = jnp.zeros((ROWS, TILE), F32)
    for s in range(source_blocks):
        for sub in range(subs):
            blocks[s, pl.ds(sub * fields, fields)] = flux_ref[sub, :, pl.ds(s * TILE, TILE)]
        atm = atm + blocks[s].astype(F32)
    acc[...] = jnp.zeros(acc.shape, F32)
    count = count_ref[0]
    me = me_ref[0]
    for copy in lists + loads:
        copy.wait()

    def slot_of(p):
        target = target_ref[p]
        half = target & 1
        owner = target >> 1
        away = (jnp.where(half == 0, owner - me, me - owner) + AHEAD) & (slots - 1)
        return jnp.where(p < count, half * slots + away, 2 * slots)

    def group(g, carry):
        terms = []
        for j in range(UNROLL):
            p = g * UNROLL + j
            terms.append(jnp.dot(blocks[source_ref[p]], bank_ref[tile_ref[p]],
                                 preferred_element_type=F32))
        for j in range(UNROLL):
            place = slot_of(g * UNROLL + j)
            acc[place] = acc[place] + terms[j]
        return carry

    lax.fori_loop(0, (count + UNROLL - 1) // UNROLL, group, 0)

    ocean = jnp.zeros((ROWS, TILE), F32)
    for half in range(2):
        for away in range(slots):
            value = acc[half * slots + away].astype(BF16)
            ocean = ocean + value.astype(F32)
            far, rest = divmod(away, FAR_STEP)
            mid, digit = divmod(rest, MID_STEP)
            place = 3 * far + mid
            if digit == 1:
                keep_ref[half, place] = value
            elif digit == 3:
                (ahead_ref, astern_ref)[half][2 * far + mid] = value
            elif (digit == 2) == (half == 0):
                right_ref[place + (0 if half == 0 else PLUS)] = value
            else:
                left_ref[place + (0 if half == 0 else MINUS)] = value
    share = 2.0 * TILE / atm_rows
    part = jnp.concatenate([atm * share - ocean, jnp.zeros((TILE - ROWS, TILE), F32)], axis=0)
    part_ref[...] = lax.dot_general(jnp.ones((8, TILE), F32), part, (((1,), (1,)), ((), ())),
                                    precision=lax.Precision.HIGHEST, preferred_element_type=F32)


def remap(pair_count, me, pair_source, pair_tile, pair_target, flux, bank, slots):
    smem = pl.BlockSpec(memory_space=pltpu.SMEM)
    vmem = pl.BlockSpec(memory_space=pltpu.VMEM)
    hbm = pl.BlockSpec(memory_space=pltpu.HBM)
    source_blocks = flux.shape[2] // TILE
    return pl.pallas_call(
        remap_kernel,
        out_shape=(jax.ShapeDtypeStruct((PLUS + MINUS, ROWS, TILE), BF16),
                   jax.ShapeDtypeStruct((PLUS + MINUS, ROWS, TILE), BF16),
                   jax.ShapeDtypeStruct((TWO, ROWS, TILE), BF16),
                   jax.ShapeDtypeStruct((TWO, ROWS, TILE), BF16),
                   jax.ShapeDtypeStruct((2, MINUS, ROWS, TILE), BF16),
                   jax.ShapeDtypeStruct((8, TILE), F32)),
        in_specs=[smem] * 2 + [hbm] * 3 + [vmem, hbm],
        out_specs=(vmem,) * 6,
        scratch_shapes=[pltpu.SMEM(pair_source.shape, jnp.int32)] * 3
        + [pltpu.VMEM(bank.shape, BF16),
           pltpu.VMEM((source_blocks, ROWS, TILE), BF16),
           pltpu.VMEM((2 * slots + 1, ROWS, TILE), F32),
           pltpu.SemaphoreType.DMA((3,)),
           pltpu.SemaphoreType.DMA((BANK_COPIES,))],
        compiler_params=pltpu.CompilerParams(vmem_limit_bytes=40 << 20),
        cost_estimate=pl.CostEstimate(flops=2 * 128 * 128 ** 3, transcendentals=0,
                                      bytes_accessed=8 << 20),
        name="remap",
    )(pair_count, me, *(pltpu.with_memory_space_constraint(x, pltpu.HBM)
                        for x in (pair_source, pair_tile, pair_target)), flux,
      pltpu.with_memory_space_constraint(bank, pltpu.HBM))


def combine_kernel(keep_ref, right_ref, left_ref, ahead_ref, astern_ref,
                   own_ref, near_ref, back_ref):
    for o in range(2):
        plus, minus = (right_ref, left_ref) if o == 0 else (left_ref, right_ref)
        for place in range(MINUS):
            far, mid = divmod(place, 3)
            value = keep_ref[o, place].astype(F32)
            if place < PLUS:
                value = value + plus[place + (0 if o == 0 else MINUS)].astype(F32)
            value = value + minus[place + (0 if o == 0 else PLUS)].astype(F32)
            if mid < 2:
                value = value + (ahead_ref, astern_ref)[o][2 * far + mid].astype(F32)
            if mid == 1:
                own_ref[o, far] = value
            elif (mid == 2) == (o == 0):
                near_ref[far + 3 * o] = value.astype(BF16)
            else:
                back_ref[far + 3 * o] = value.astype(BF16)


def combine(keep, right, left, ahead, astern):
    vmem = pl.BlockSpec(memory_space=pltpu.VMEM)
    sent = jax.ShapeDtypeStruct((6, ROWS, TILE), BF16)
    return pl.pallas_call(
        combine_kernel,
        out_shape=(jax.ShapeDtypeStruct((2, 3, ROWS, TILE), F32), sent, sent),
        in_specs=[vmem] * 5,
        out_specs=(vmem,) * 3,
        compiler_params=pltpu.CompilerParams(vmem_limit_bytes=16 << 20),
        name="combine",
    )(keep, right, left, ahead, astern)


def gather_kernel(own_ref, near_ref, back_ref, rest_ref, plus_ref, minus_ref):
    for o in range(2):
        for far in range(3):
            value = (own_ref[o, far] + near_ref[far + 3 * o].astype(F32)
                     + back_ref[far + 3 * o].astype(F32))
            if far == 1:
                rest_ref[o] = value
                continue
            sent = value.astype(BF16)
            if (far == 2) == (o == 0):
                plus_ref[o] = sent
            else:
                minus_ref[o] = sent


def gather(own, near, back):
    vmem = pl.BlockSpec(memory_space=pltpu.VMEM)
    pair = jax.ShapeDtypeStruct((2, ROWS, TILE), BF16)
    return pl.pallas_call(
        gather_kernel,
        out_shape=(jax.ShapeDtypeStruct((2, ROWS, TILE), F32), pair, pair),
        in_specs=[vmem] * 3,
        out_specs=(vmem,) * 3,
        compiler_params=pltpu.CompilerParams(vmem_limit_bytes=16 << 20),
        name="gather",
    )(own, near, back)


def mix_kernel(tracer_ref, diff_ref, depth_ref, solved_ref, unit_ref, state_ref, ahead, lower, upper):
    levels, fields, columns = tracer_ref.shape
    depth = depth_ref[...]
    zero = jnp.zeros((1, columns), F32)
    one = jnp.ones((1, columns), F32)

    def coupling(k):
        if k == 0 or k == levels:
            return zero
        return jnp.where(depth > k, diff_ref[pl.ds(k - 1, 1), :], zero)

    ratio = None
    for k in range(levels):
        a, b = coupling(k), coupling(k + 1)
        pivot = 1.0 + a + b
        if k > 0:
            pivot = pivot - a * ratio
        inverse = 1.0 / pivot
        ratio = b * inverse
        wet = jnp.where(depth > k, one, zero)
        ahead[pl.ds(k, 1), :] = wet * inverse
        lower[pl.ds(k, 1), :] = a * inverse
        upper[pl.ds(k, 1), :] = ratio
    unit = [jnp.where(depth > 0, one, zero)] + [zero] * (levels - 1)
    for sweep in range(2):
        carried = None
        unit_carried = None
        for k in range(levels):
            if sweep == 0:
                x = tracer_ref[k].astype(F32)
            else:
                x = state_ref[k]
            scale = ahead[pl.ds(k, 1), :]
            below = lower[pl.ds(k, 1), :]
            if k == 0:
                carried = x * scale
                unit_carried = unit[k] * scale
            else:
                carried = x * scale + carried * below
                unit_carried = unit[k] * scale + unit_carried * below
            if sweep == 1 and k == levels - 1:
                solved_ref[:, k, :] = carried
            else:
                state_ref[k] = carried
            unit[k] = unit_carried
        for k in range(levels - 2, -1, -1):
            above = upper[pl.ds(k, 1), :]
            carried = state_ref[k] + carried * above
            if sweep == 1:
                solved_ref[:, k, :] = carried
            else:
                state_ref[k] = carried
            unit[k] = unit[k] + unit[k + 1] * above
        for k in range(levels):
            unit_ref[sweep, pl.ds(k, 1), :] = unit[k]


def mix(tracers, diffusivity, column_depth):
    levels, fields, columns = tracers.shape
    vmem = pl.BlockSpec(memory_space=pltpu.VMEM)
    return pl.pallas_call(
        mix_kernel,
        out_shape=(jax.ShapeDtypeStruct((fields, levels, columns), F32),
                   jax.ShapeDtypeStruct((2, levels, columns), F32)),
        in_specs=[vmem] * 3,
        out_specs=(vmem, vmem),
        scratch_shapes=[pltpu.VMEM(tracers.shape, F32)] + [pltpu.VMEM((levels, columns), F32)] * 3,
        compiler_params=pltpu.CompilerParams(vmem_limit_bytes=24 << 20),
        cost_estimate=pl.CostEstimate(flops=12 * levels * fields * columns, transcendentals=0,
                                      bytes_accessed=6 * levels * fields * columns),
        name="mix",
    )(tracers, diffusivity, column_depth.reshape(1, columns))


def finish_kernel(scale, state_ref, unit_ref, rest_ref, plus_ref, minus_ref,
                  total_ref, out_hbm,
                  surface, result, sems):
    fields, levels, columns = state_ref.shape
    eye = (lax.broadcasted_iota(jnp.int32, (ROWS, TILE), 0)
           == lax.broadcasted_iota(jnp.int32, (ROWS, TILE), 1))
    total = total_ref[...] * scale
    spread = jnp.where(eye, jnp.broadcast_to(total, (ROWS, TILE)), 0.0)
    fix = jnp.sum(spread, axis=1, keepdims=True)
    for o in range(2):
        surface[:, pl.ds(o * TILE, TILE)] = (rest_ref[o] + plus_ref[o].astype(F32)
                                             + minus_ref[o].astype(F32)) + fix
    once = unit_ref[0]
    twice = unit_ref[1]
    copies = []
    for start in range(0, fields, FIELD_CHUNK):
        for f in range(start, start + FIELD_CHUNK):
            result[f] = (state_ref[f] + surface[pl.ds(f, 1), :] * twice
                         + surface[pl.ds(fields + f, 1), :] * once)
        part = pl.ds(start, FIELD_CHUNK)
        copies.append(pltpu.make_async_copy(result.at[part], out_hbm.at[part],
                                            sems.at[start // FIELD_CHUNK]))
        copies[-1].start()
    for copy in copies:
        copy.wait()


def finish(state, unit, rest, plus, minus, total, scale):
    vmem = pl.BlockSpec(memory_space=pltpu.VMEM)
    fields, levels, columns = state.shape
    return pl.pallas_call(
        functools.partial(finish_kernel, scale),
        out_shape=jax.ShapeDtypeStruct(state.shape, F32),
        in_specs=[vmem] * 6,
        out_specs=pl.BlockSpec(memory_space=pltpu.HBM),
        scratch_shapes=[pltpu.VMEM((ROWS, columns), F32), pltpu.VMEM(state.shape, F32),
                        pltpu.SemaphoreType.DMA((fields // FIELD_CHUNK,))],
        compiler_params=pltpu.CompilerParams(vmem_limit_bytes=24 << 20),
        name="finish",
    )(state, unit, rest, plus, minus, total)


def shift(x, by, ring):
    return lax.ppermute(x, "blk", [(i, (i + by) % ring) for i in range(ring)])


def body(
    atm_flux,
    tile_bank,
    pair_count,
    pair_source,
    pair_tile,
    pair_target,
    tracers,
    diffusivity,
    column_depth,
):
    ring = lax.axis_size("blk")
    plane = lax.axis_size("sec") * lax.axis_size("grp")
    columns = tracers.shape[2]
    me = lax.axis_index("blk").astype(jnp.int32).reshape(1)
    right, left, ahead, astern, keep, part = remap(
        pair_count, me, pair_source, pair_tile, pair_target, atm_flux, tile_bank, ring)
    ahead = shift(ahead, 2, ring)
    astern = shift(astern, -2, ring)
    right = shift(right, 1, ring)
    left = shift(left, -1, ring)
    gathered = lax.all_to_all(jnp.broadcast_to(part[:1], (plane, TILE)), ("sec", "grp"), 0, 0,
                              tiled=True)
    gathered, right = lax.optimization_barrier((gathered, right))
    own, near, back = combine(keep, right, left, ahead, astern)
    near = shift(near, MID_STEP, ring)
    back = shift(back, -MID_STEP, ring)
    gathered, own = lax.optimization_barrier((gathered, own))
    group = ring // 2
    total = jnp.broadcast_to(jnp.sum(gathered, axis=0, keepdims=True), (group, TILE))
    total = lax.all_to_all(total, "blk", 0, 0, tiled=True,
                           axis_index_groups=[list(range(group)), list(range(group, ring))])
    rest, plus, minus = gather(own, near, back)
    column_depth, rest = lax.optimization_barrier((column_depth, rest))
    state, unit = mix(tracers, diffusivity, column_depth)
    total, unit = lax.optimization_barrier((total, unit))
    total = jnp.sum(total, axis=0, keepdims=True)
    plus = shift(plus, FAR_STEP, ring)
    minus = shift(minus, -FAR_STEP, ring)
    total = lax.all_to_all(jnp.concatenate([total, total], axis=0), "blk", 0, 0, tiled=True,
                           axis_index_groups=[[i, ring - 1 - i] for i in range(group)])
    total = jnp.sum(total, axis=0, keepdims=True)
    result = finish(state, unit, rest, plus, minus, total, 1.0 / (columns * ring * plane))
    return jnp.transpose(result, (1, 0, 2))


def solution(mesh):
    placed = (
        P(None, None, ("sec", "grp", "blk")),
        P(),
        P(("sec", "grp", "blk")),
        P(("sec", "grp", "blk")),
        P(("sec", "grp", "blk")),
        P(("sec", "grp", "blk")),
        P(None, None, ("sec", "grp", "blk")),
        P(None, ("sec", "grp", "blk")),
        P(("sec", "grp", "blk")),
    )
    return jax.shard_map(
        body,
        mesh=mesh,
        in_specs=placed,
        out_specs=P(None, None, ("sec", "grp", "blk")),
        check_vma=False,
    )
```

```python
import functools

import jax
import jax.numpy as jnp
from jax import lax
from jax.experimental import pallas as pl
from jax.experimental.pallas import tpu as pltpu
from jax.sharding import PartitionSpec as P

F32 = jnp.float32
BF16 = jnp.bfloat16
ROWS = 120
TILE = 128
UNROLL = 8
BANK_COPIES = 8
FIELD_CHUNK = 15
FAR_STEP = 11
MID_STEP = 4
AHEAD = FAR_STEP + MID_STEP + 1
PLUS = 8
MINUS = 9
TWO = 6


def remap_kernel(count_ref, me_ref, source_hbm, tile_hbm, target_hbm, flux_ref, bank_hbm,
                 right_ref, left_ref, ahead_ref, astern_ref, keep_ref, part_ref,
                 source_ref, tile_ref, target_ref, bank_ref, blocks, acc, list_sem, bank_sem):
    subs, fields, atm_rows = flux_ref.shape
    source_blocks = atm_rows // TILE
    slots = (acc.shape[0] - 1) // 2
    lists = [pltpu.make_async_copy(src, dst, list_sem.at[i]) for i, (src, dst) in enumerate(
        ((source_hbm, source_ref), (tile_hbm, tile_ref), (target_hbm, target_ref)))]
    span = bank_ref.shape[0] // BANK_COPIES
    loads = [pltpu.make_async_copy(bank_hbm.at[pl.ds(i * span, span)],
                                   bank_ref.at[pl.ds(i * span, span)], bank_sem.at[i])
             for i in range(BANK_COPIES)]
    for copy in lists + loads:
        copy.start()
    blocks[...] = jnp.zeros(blocks.shape, BF16)
    atm = jnp.zeros((ROWS, TILE), F32)
    for s in range(source_blocks):
        for sub in range(subs):
            blocks[s, pl.ds(sub * fields, fields)] = flux_ref[sub, :, pl.ds(s * TILE, TILE)]
        atm = atm + blocks[s].astype(F32)
    acc[...] = jnp.zeros(acc.shape, F32)
    count = count_ref[0]
    me = me_ref[0]
    for copy in lists + loads:
        copy.wait()

    def slot_of(p):
        target = target_ref[p]
        half = target & 1
        owner = target >> 1
        away = (jnp.where(half == 0, owner - me, me - owner) + AHEAD) & (slots - 1)
        return jnp.where(p < count, half * slots + away, 2 * slots)

    def group(g, carry):
        terms = []
        for j in range(UNROLL):
            p = g * UNROLL + j
            terms.append(jnp.dot(blocks[source_ref[p]], bank_ref[tile_ref[p]],
                                 preferred_element_type=F32))
        for j in range(UNROLL):
            place = slot_of(g * UNROLL + j)
            acc[place] = acc[place] + terms[j]
        return carry

    lax.fori_loop(0, (count + UNROLL - 1) // UNROLL, group, 0)

    ocean = jnp.zeros((ROWS, TILE), F32)
    for half in range(2):
        for away in range(slots):
            value = acc[half * slots + away].astype(BF16)
            ocean = ocean + value.astype(F32)
            far, rest = divmod(away, FAR_STEP)
            mid, digit = divmod(rest, MID_STEP)
            place = 3 * far + mid
            if digit == 1:
                keep_ref[half, place] = value
            elif digit == 3:
                (ahead_ref, astern_ref)[half][2 * far + mid] = value
            elif (digit == 2) == (half == 0):
                right_ref[place + (0 if half == 0 else PLUS)] = value
            else:
                left_ref[place + (0 if half == 0 else MINUS)] = value
    share = 2.0 * TILE / atm_rows
    part = jnp.concatenate([atm * share - ocean, jnp.zeros((TILE - ROWS, TILE), F32)], axis=0)
    part_ref[...] = lax.dot_general(jnp.ones((8, TILE), F32), part, (((1,), (1,)), ((), ())),
                                    precision=lax.Precision.HIGHEST, preferred_element_type=F32)


def remap(pair_count, me, pair_source, pair_tile, pair_target, flux, bank, slots):
    smem = pl.BlockSpec(memory_space=pltpu.SMEM)
    vmem = pl.BlockSpec(memory_space=pltpu.VMEM)
    hbm = pl.BlockSpec(memory_space=pltpu.HBM)
    source_blocks = flux.shape[2] // TILE
    return pl.pallas_call(
        remap_kernel,
        out_shape=(jax.ShapeDtypeStruct((PLUS + MINUS, ROWS, TILE), BF16),
                   jax.ShapeDtypeStruct((PLUS + MINUS, ROWS, TILE), BF16),
                   jax.ShapeDtypeStruct((TWO, ROWS, TILE), BF16),
                   jax.ShapeDtypeStruct((TWO, ROWS, TILE), BF16),
                   jax.ShapeDtypeStruct((2, MINUS, ROWS, TILE), BF16),
                   jax.ShapeDtypeStruct((8, TILE), F32)),
        in_specs=[smem] * 2 + [hbm] * 3 + [vmem, hbm],
        out_specs=(vmem,) * 6,
        scratch_shapes=[pltpu.SMEM(pair_source.shape, jnp.int32)] * 3
        + [pltpu.VMEM(bank.shape, BF16),
           pltpu.VMEM((source_blocks, ROWS, TILE), BF16),
           pltpu.VMEM((2 * slots + 1, ROWS, TILE), F32),
           pltpu.SemaphoreType.DMA((3,)),
           pltpu.SemaphoreType.DMA((BANK_COPIES,))],
        compiler_params=pltpu.CompilerParams(vmem_limit_bytes=40 << 20),
        cost_estimate=pl.CostEstimate(flops=2 * 128 * 128 ** 3, transcendentals=0,
                                      bytes_accessed=8 << 20),
        name="remap",
    )(pair_count, me, *(pltpu.with_memory_space_constraint(x, pltpu.HBM)
                        for x in (pair_source, pair_tile, pair_target)), flux,
      pltpu.with_memory_space_constraint(bank, pltpu.HBM))


def combine_kernel(keep_ref, right_ref, left_ref, ahead_ref, astern_ref,
                   own_ref, near_ref, back_ref):
    for o in range(2):
        plus, minus = (right_ref, left_ref) if o == 0 else (left_ref, right_ref)
        for place in range(MINUS):
            far, mid = divmod(place, 3)
            value = keep_ref[o, place].astype(F32)
            if place < PLUS:
                value = value + plus[place + (0 if o == 0 else MINUS)].astype(F32)
            value = value + minus[place + (0 if o == 0 else PLUS)].astype(F32)
            if mid < 2:
                value = value + (ahead_ref, astern_ref)[o][2 * far + mid].astype(F32)
            if mid == 1:
                own_ref[o, far] = value
            elif (mid == 2) == (o == 0):
                near_ref[far + 3 * o] = value.astype(BF16)
            else:
                back_ref[far + 3 * o] = value.astype(BF16)


def combine(keep, right, left, ahead, astern):
    vmem = pl.BlockSpec(memory_space=pltpu.VMEM)
    sent = jax.ShapeDtypeStruct((6, ROWS, TILE), BF16)
    return pl.pallas_call(
        combine_kernel,
        out_shape=(jax.ShapeDtypeStruct((2, 3, ROWS, TILE), F32), sent, sent),
        in_specs=[vmem] * 5,
        out_specs=(vmem,) * 3,
        compiler_params=pltpu.CompilerParams(vmem_limit_bytes=16 << 20),
        name="combine",
    )(keep, right, left, ahead, astern)


def gather_kernel(own_ref, near_ref, back_ref, rest_ref, plus_ref, minus_ref):
    for o in range(2):
        for far in range(3):
            value = (own_ref[o, far] + near_ref[far + 3 * o].astype(F32)
                     + back_ref[far + 3 * o].astype(F32))
            if far == 1:
                rest_ref[o] = value
                continue
            sent = value.astype(BF16)
            if (far == 2) == (o == 0):
                plus_ref[o] = sent
            else:
                minus_ref[o] = sent


def gather(own, near, back):
    vmem = pl.BlockSpec(memory_space=pltpu.VMEM)
    pair = jax.ShapeDtypeStruct((2, ROWS, TILE), BF16)
    return pl.pallas_call(
        gather_kernel,
        out_shape=(jax.ShapeDtypeStruct((2, ROWS, TILE), F32), pair, pair),
        in_specs=[vmem] * 3,
        out_specs=(vmem,) * 3,
        compiler_params=pltpu.CompilerParams(vmem_limit_bytes=16 << 20),
        name="gather",
    )(own, near, back)


def mix_kernel(tracer_ref, diff_ref, depth_ref, solved_ref, unit_ref, state_ref, ahead, lower, upper):
    levels, fields, columns = tracer_ref.shape
    depth = depth_ref[...]
    zero = jnp.zeros((1, columns), F32)
    one = jnp.ones((1, columns), F32)

    def coupling(k):
        if k == 0 or k == levels:
            return zero
        return jnp.where(depth > k, diff_ref[pl.ds(k - 1, 1), :], zero)

    ratio = None
    for k in range(levels):
        a, b = coupling(k), coupling(k + 1)
        pivot = 1.0 + a + b
        if k > 0:
            pivot = pivot - a * ratio
        inverse = 1.0 / pivot
        ratio = b * inverse
        wet = jnp.where(depth > k, one, zero)
        ahead[pl.ds(k, 1), :] = wet * inverse
        lower[pl.ds(k, 1), :] = a * inverse
        upper[pl.ds(k, 1), :] = ratio
    unit = [jnp.where(depth > 0, one, zero)] + [zero] * (levels - 1)
    for sweep in range(2):
        carried = None
        unit_carried = None
        for k in range(levels):
            if sweep == 0:
                x = tracer_ref[k].astype(F32)
            else:
                x = state_ref[k]
            scale = ahead[pl.ds(k, 1), :]
            below = lower[pl.ds(k, 1), :]
            if k == 0:
                carried = x * scale
                unit_carried = unit[k] * scale
            else:
                carried = x * scale + carried * below
                unit_carried = unit[k] * scale + unit_carried * below
            if sweep == 1 and k == levels - 1:
                solved_ref[:, k, :] = carried
            else:
                state_ref[k] = carried
            unit[k] = unit_carried
        for k in range(levels - 2, -1, -1):
            above = upper[pl.ds(k, 1), :]
            carried = state_ref[k] + carried * above
            if sweep == 1:
                solved_ref[:, k, :] = carried
            else:
                state_ref[k] = carried
            unit[k] = unit[k] + unit[k + 1] * above
        for k in range(levels):
            unit_ref[sweep, pl.ds(k, 1), :] = unit[k]


def mix(tracers, diffusivity, column_depth):
    levels, fields, columns = tracers.shape
    vmem = pl.BlockSpec(memory_space=pltpu.VMEM)
    return pl.pallas_call(
        mix_kernel,
        out_shape=(jax.ShapeDtypeStruct((fields, levels, columns), F32),
                   jax.ShapeDtypeStruct((2, levels, columns), F32)),
        in_specs=[vmem] * 3,
        out_specs=(vmem, vmem),
        scratch_shapes=[pltpu.VMEM(tracers.shape, F32)] + [pltpu.VMEM((levels, columns), F32)] * 3,
        compiler_params=pltpu.CompilerParams(vmem_limit_bytes=24 << 20),
        cost_estimate=pl.CostEstimate(flops=12 * levels * fields * columns, transcendentals=0,
                                      bytes_accessed=6 * levels * fields * columns),
        name="mix",
    )(tracers, diffusivity, column_depth.reshape(1, columns))


def finish_kernel(scale, state_ref, unit_ref, rest_ref, plus_ref, minus_ref,
                  total_ref, out_hbm,
                  surface, result, sems):
    fields, levels, columns = state_ref.shape
    eye = (lax.broadcasted_iota(jnp.int32, (ROWS, TILE), 0)
           == lax.broadcasted_iota(jnp.int32, (ROWS, TILE), 1))
    total = total_ref[...] * scale
    spread = jnp.where(eye, jnp.broadcast_to(total, (ROWS, TILE)), 0.0)
    fix = jnp.sum(spread, axis=1, keepdims=True)
    for o in range(2):
        surface[:, pl.ds(o * TILE, TILE)] = (rest_ref[o] + plus_ref[o].astype(F32)
                                             + minus_ref[o].astype(F32)) + fix
    once = unit_ref[0]
    twice = unit_ref[1]
    copies = []
    for start in range(0, fields, FIELD_CHUNK):
        for f in range(start, start + FIELD_CHUNK):
            result[f] = (state_ref[f] + surface[pl.ds(f, 1), :] * twice
                         + surface[pl.ds(fields + f, 1), :] * once)
        part = pl.ds(start, FIELD_CHUNK)
        copies.append(pltpu.make_async_copy(result.at[part], out_hbm.at[part],
                                            sems.at[start // FIELD_CHUNK]))
        copies[-1].start()
    for copy in copies:
        copy.wait()


def finish(state, unit, rest, plus, minus, total, scale):
    vmem = pl.BlockSpec(memory_space=pltpu.VMEM)
    fields, levels, columns = state.shape
    return pl.pallas_call(
        functools.partial(finish_kernel, scale),
        out_shape=jax.ShapeDtypeStruct(state.shape, F32),
        in_specs=[vmem] * 6,
        out_specs=pl.BlockSpec(memory_space=pltpu.HBM),
        scratch_shapes=[pltpu.VMEM((ROWS, columns), F32), pltpu.VMEM(state.shape, F32),
                        pltpu.SemaphoreType.DMA((fields // FIELD_CHUNK,))],
        compiler_params=pltpu.CompilerParams(vmem_limit_bytes=24 << 20),
        name="finish",
    )(state, unit, rest, plus, minus, total)


def shift(x, by, ring):
    return lax.ppermute(x, "blk", [(i, (i + by) % ring) for i in range(ring)])


def body(
    atm_flux,
    tile_bank,
    pair_count,
    pair_source,
    pair_tile,
    pair_target,
    tracers,
    diffusivity,
    column_depth,
):
    ring = lax.axis_size("blk")
    plane = lax.axis_size("sec") * lax.axis_size("grp")
    columns = tracers.shape[2]
    me = lax.axis_index("blk").astype(jnp.int32).reshape(1)
    right, left, ahead, astern, keep, part = remap(
        pair_count, me, pair_source, pair_tile, pair_target, atm_flux, tile_bank, ring)
    ahead = shift(ahead, 2, ring)
    astern = shift(astern, -2, ring)
    right = shift(right, 1, ring)
    left = shift(left, -1, ring)
    gathered = lax.all_to_all(jnp.broadcast_to(part[:1], (plane, TILE)), ("sec", "grp"), 0, 0,
                              tiled=True)
    gathered, right = lax.optimization_barrier((gathered, right))
    own, near, back = combine(keep, right, left, ahead, astern)
    near = shift(near, MID_STEP, ring)
    back = shift(back, -MID_STEP, ring)
    gathered, own = lax.optimization_barrier((gathered, own))
    group = ring // 4
    total = jnp.broadcast_to(jnp.sum(gathered, axis=0, keepdims=True), (group, TILE))
    total = lax.all_to_all(total, "blk", 0, 0, tiled=True,
                           axis_index_groups=[[g * group + i for i in range(group)]
                                              for g in range(4)])
    total, near = lax.optimization_barrier((total, near))
    rest, plus, minus = gather(own, near, back)
    column_depth, rest = lax.optimization_barrier((column_depth, rest))
    state, unit = mix(tracers, diffusivity, column_depth)
    total, unit = lax.optimization_barrier((total, unit))
    total = jnp.sum(total, axis=0, keepdims=True)
    plus = shift(plus, FAR_STEP, ring)
    minus = shift(minus, -FAR_STEP, ring)
    total = lax.all_to_all(jnp.concatenate([total] * 4, axis=0), "blk", 0, 0, tiled=True,
                           axis_index_groups=[[i, 2 * group - 1 - i, 2 * group + i, ring - 1 - i]
                                              for i in range(group)])
    total = jnp.sum(total, axis=0, keepdims=True)
    result = finish(state, unit, rest, plus, minus, total, 1.0 / (columns * ring * plane))
    return jnp.transpose(result, (1, 0, 2))


def solution(mesh):
    placed = (
        P(None, None, ("sec", "grp", "blk")),
        P(),
        P(("sec", "grp", "blk")),
        P(("sec", "grp", "blk")),
        P(("sec", "grp", "blk")),
        P(("sec", "grp", "blk")),
        P(None, None, ("sec", "grp", "blk")),
        P(None, ("sec", "grp", "blk")),
        P(("sec", "grp", "blk")),
    )
    return jax.shard_map(
        body,
        mesh=mesh,
        in_specs=placed,
        out_specs=P(None, None, ("sec", "grp", "blk")),
        check_vma=False,
    )
```
